128 devices in a mesh: gx: 32 (over y_lo, x, z), gy: 4 (over y_hi, core).
Axes of the slice: x: 4, y: 4 (y_hi: 2, y_lo: 2; y = y_hi * 2 + y_lo), z: 4, core: 2. Of those that a mesh axis runs over, the one named last changes fastest.
Arguments:
- electric: float32 [3, 128, 96, 512], P(None, 'gx', None, 'gy'), may hold values from -6 to 6
- magnetic: float32 [3, 128, 96, 512], P(None, 'gx', None, 'gy'), may hold values from -6 to 6
- polarization: float32 [3, 128, 96, 512], P(None, 'gx', None, 'gy'), may hold values from -6 to 6
- current: float32 [3, 128, 96, 512], P(None, 'gx', None, 'gy'), may hold values from -6 to 6
- inversion: float32 [128, 96, 512], P('gx', None, 'gy'), may hold values from -1 to 1
- gain_mask: int32 [128, 96, 512], P('gx', None, 'gy'), may hold values 0 or 1
- pump_region: int32 [128, 96, 512], P('gx', None, 'gy'), may hold values from 0 to 7
- pump_level: float32 [8], replicated, may hold values from -0.5 to 2
Outputs:
- final_field: float32 [3, 128, 96, 512], P(None, 'gx', None, 'gy')
- far_field: float32 [64, 16, 512], P('gx', 'gy')
The draws below stay inside these ranges and needn't reach their ends.
All inputs are finite; a program needn't handle non-finite values. No bound on the sum of `gain_mask` on one device may be relied on, other than what follows from the above.
Results may differ from the reference program's by a relative error of at most 0.0003.
Values sent between devices are 32-bit elements; how exact they have to be, the bound alone decides.
A program may use at most 64 MiB of HBM per device.

```python
import math
import jax
import jax.numpy as jnp
from jax import lax

NZ = 96
STEPS = 4
NF = 16
NUX = 64
NUY = 64
REGIONS = 8
NX = 128
NY = 512


def plant(result, own_key, smallest, high):
    longest = result.shape.index(max(result.shape))
    spots = []
    for shift in (0, 1):
        where = [jax.random.randint(jax.random.fold_in(own_key, axis), (), 0, length) for axis, length in enumerate(result.shape)]
        where[longest] = (where[longest] + shift) % result.shape[longest]
        spots.append(tuple(where))
    return result.at[spots[0]].set(smallest).at[spots[1]].set(high)


def block_levels(key, shape, split, low, largest):
    loudness = 1.0
    for axis_at, parts in split:
        steps = jax.random.uniform(jax.random.fold_in(jax.random.fold_in(key, 6), axis_at), (parts,), jnp.float32, low / len(split), largest / len(split))
        loudness = loudness * jnp.repeat(jnp.exp(steps), shape[axis_at] // parts).reshape((-1,) + (1,) * (len(shape) - 1 - axis_at))
    return loudness


def normal_values(rng, shape, width, bound, shards=(), held_as=jnp.bfloat16):
    result = jax.random.normal(rng, shape, jnp.float32) * width
    if len(shards) > 0:
        result = block_levels(rng, shape, shards, -0.22, 0.18) * result
    return jnp.clip(result, min=-bound, max=bound).astype(held_as)


def setup_inputs(seed: int = 0) -> dict:
    key_list = jax.random.split(jax.random.key(seed), 9)
    return {
        "electric": normal_values(key_list[0], (3, NX, NZ, NY), 1.0, 6.0, ((1, 32), (3, 4)), jnp.float32),
        "magnetic": normal_values(key_list[1], (3, NX, NZ, NY), 1.0, 6.0, ((1, 32), (3, 4)), jnp.float32),
        "polarization": normal_values(key_list[2], (3, NX, NZ, NY), 1.0, 6.0, ((1, 32), (3, 4)), jnp.float32),
        "current": normal_values(key_list[3], (3, NX, NZ, NY), 1.0, 6.0, ((1, 32), (3, 4)), jnp.float32),
        "inversion": jnp.clip(jax.random.uniform(key_list[4], (NX, NZ, NY), jnp.float32, -1.0, 1.0) * block_levels(key_list[4], (NX, NZ, NY), ((0, 32), (2, 4)), -0.4, 0.0), -1.0, 1.0),
        "gain_mask": plant((jax.random.randint(key_list[5], (NX, NZ, NY), 0, 2) < 1).astype(jnp.int32), jax.random.fold_in(key_list[5], 1), 0, 1),
        "pump_region": plant(jax.random.randint(key_list[6], (NX, NZ, NY), 0, REGIONS), jax.random.fold_in(key_list[6], 1), 0, REGIONS - 1).astype(jnp.int32),
        "pump_level": jnp.clip(jax.random.uniform(key_list[7], (REGIONS,), jnp.float32, -0.5, 2.0), -0.5, 2.0),
    }


time_step = 0.5
damping = 0.4
omega_zero = 1.0
coupling = 1.0
saturation = 0.5
recovery = 0.8
freq_base = 0.6
freq_step = 0.05
spread_cosine = 0.75

def magnetic_update(magnetic, electric_ext):
    field_x, field_y, field_z = (electric_ext[0], electric_ext[1], electric_ext[2])

    def central(value):
        return value[:-1, :, :-1]

    def delta_x(value):
        return value[1:, :, :-1] - value[:-1, :, :-1]

    def delta_y(value):
        return value[:-1, :, 1:] - value[:-1, :, :-1]

    def delta_z(value):
        middle = central(value)
        shifted = jnp.concatenate([middle[:, 1:, :], jnp.zeros_like(middle[:, :1, :])], axis=1)
        return shifted - middle
    curl = jnp.stack([delta_y(field_z) - delta_z(field_y), delta_z(field_x) - delta_x(field_z), delta_x(field_y) - delta_y(field_x)])
    return magnetic - time_step * curl

def electric_curl(magnetic_ext):
    field_x, field_y, field_z = (magnetic_ext[0], magnetic_ext[1], magnetic_ext[2])

    def central(value):
        return value[1:, :, 1:]

    def delta_x(value):
        return value[1:, :, 1:] - value[:-1, :, 1:]

    def delta_y(value):
        return value[1:, :, 1:] - value[1:, :, :-1]

    def delta_z(value):
        middle = central(value)
        shifted = jnp.concatenate([jnp.zeros_like(middle[:, :1, :]), middle[:, :-1, :]], axis=1)
        return middle - shifted
    return jnp.stack([delta_y(field_z) - delta_z(field_y), delta_z(field_x) - delta_x(field_z), delta_x(field_y) - delta_y(field_x)])

def bloch_update(electric, curl_field, polarization, current, inversion, gain_cells, pump_rate):
    driven = (1.0 - 0.5 * damping * time_step) * current + time_step * (coupling * inversion[None] * electric - omega_zero * omega_zero * polarization)
    current_new = gain_cells[None] * driven / (1.0 + 0.5 * damping * time_step)
    polar_new = polarization + time_step * current_new
    electric_new = electric + time_step * (curl_field - current_new)
    absorbed = 0.5 * lax.optimization_barrier(jnp.sum((electric + electric_new) * current_new, axis=0))
    inversion_new = inversion + time_step * (recovery * (pump_rate - inversion) - saturation * absorbed)
    return (electric_new, polar_new, current_new, inversion_new)

def frequencies_from(first, count):
    return freq_base + freq_step * (first + jnp.arange(count)).astype(jnp.float32)

def directions(count, first, rows):
    places = (first + jnp.arange(rows)).astype(jnp.float32)
    return spread_cosine * (2.0 * places - (count - 1)) / (count - 1)

def accumulate(real, imag, top, moment, count):
    phase = frequencies_from(0, count) * moment
    real = real + (time_step * jnp.cos(phase))[:, None, None, None] * top[None]
    imag = imag + (-time_step * jnp.sin(phase))[:, None, None, None] * top[None]
    return (real, imag)

def product(form, left, right):
    return jnp.einsum(form, left, right, precision=lax.Precision.HIGHEST, preferred_element_type=jnp.float32)

def contract_y(spectra, wavenumber, places):
    cosines = directions(NUY, 0, NUY)
    phase = (wavenumber[:, None] * cosines[None, :])[:, :, None] * places[None, None, :]
    cos_table = jnp.cos(phase)
    sin_table = jnp.sin(phase)
    real_part = spectra[:, :4]
    imag_part = spectra[:, 4:]
    inner_real = product('fcxy,fby->fcxb', real_part, cos_table) - product('fcxy,fby->fcxb', imag_part, sin_table)
    inner_imag = product('fcxy,fby->fcxb', real_part, sin_table) + product('fcxy,fby->fcxb', imag_part, cos_table)
    return jnp.concatenate([inner_real, inner_imag], axis=1)

def contract_x(inner, wavenumber, stations, first, rows):
    cosines = directions(NUX, first, rows)
    phase = (wavenumber[:, None] * cosines[None, :])[:, :, None] * stations[None, None, :]
    cos_rows = jnp.cos(phase)
    sin_rows = jnp.sin(phase)
    inner_real = inner[:, :4]
    inner_imag = inner[:, 4:]
    outer_real = product('fax,fcxb->afcb', cos_rows, inner_real) - product('fax,fcxb->afcb', sin_rows, inner_imag)
    outer_imag = product('fax,fcxb->afcb', sin_rows, inner_real) + product('fax,fcxb->afcb', cos_rows, inner_imag)
    joined = jnp.concatenate([outer_real, outer_imag], axis=2)
    return joined.reshape(rows, joined.shape[1], 8 * NUY)

def reference(electric, magnetic, polarization, current, inversion, gain_mask, pump_region, pump_level):
    gain_cells = gain_mask.astype(jnp.float32)
    pump_rate = pump_level[pump_region]
    plane = (NF, 2, NX, NY)
    h_real = jnp.zeros(plane, jnp.float32)
    h_imag = jnp.zeros(plane, jnp.float32)
    e_real = jnp.zeros(plane, jnp.float32)
    e_imag = jnp.zeros(plane, jnp.float32)
    for iteration in range(STEPS):
        electric_ext = jnp.pad(electric, ((0, 0), (0, 1), (0, 0), (0, 1)))
        magnetic = magnetic_update(magnetic, electric_ext)
        top_h = jnp.stack([-magnetic[1, :, -1, :], magnetic[0, :, -1, :]])
        h_real, h_imag = accumulate(h_real, h_imag, top_h, (iteration + 0.5) * time_step, NF)
        magnetic_ext = jnp.pad(magnetic, ((0, 0), (1, 0), (0, 0), (1, 0)))
        electric, polarization, current, inversion = bloch_update(electric, electric_curl(magnetic_ext), polarization, current, inversion, gain_cells, pump_rate)
        top_e = jnp.stack([electric[1, :, -1, :], -electric[0, :, -1, :]])
        e_real, e_imag = accumulate(e_real, e_imag, top_e, (iteration + 1.0) * time_step, NF)
    spectra = jnp.concatenate([h_real, e_real, h_imag, e_imag], axis=1)
    wavenumber = frequencies_from(0, NF)
    places = jnp.arange(NY).astype(jnp.float32) - NY / 2
    stations = jnp.arange(NX).astype(jnp.float32) - NX / 2
    inner = contract_y(spectra, wavenumber, places)
    far_field = contract_x(inner, wavenumber, stations, 0, NUX) * (1.0 / math.sqrt(NX * NY))
    return (electric, far_field)
```

```python
import functools
import math

import jax
import jax.numpy as jnp
from jax import lax
from jax.experimental import pallas as pl
from jax.experimental.pallas import tpu as pltpu
from jax.sharding import PartitionSpec as P

MESH = pl.DeviceIdType.MESH
F32 = jnp.float32
BF16 = jnp.bfloat16

STEPS = 4
NZ = 96
LX = 4
LANES = 128
CH = 32
NCH = NZ // CH
FL = 4

DT = 0.5
DAMP = 0.4
SAT = 0.5
REC = 0.8
C_DEN = 1.0 + 0.5 * DAMP * DT
C_J = (1.0 - 0.5 * DAMP * DT) / C_DEN
C_D = DT / C_DEN


def sin_turns(turns):
    r = turns - jnp.floor(turns + 0.5)
    x = r * (2.0 * math.pi)
    s = x * x
    acc = jnp.full_like(s, 1.0 / math.factorial(17))
    for order, sign in ((15, -1.0), (13, 1.0), (11, -1.0), (9, 1.0), (7, -1.0), (5, 1.0), (3, -1.0), (1, 1.0)):
        acc = acc * s + sign / math.factorial(order)
    return acc * x


def split(value):
    high = value.astype(BF16)
    return high, (value - high.astype(F32)).astype(BF16)


def dot3(a, b):
    ah, al = a
    bh, bl = b
    dot = functools.partial(jnp.dot, preferred_element_type=F32)
    return dot(ah, bh) + dot(al, bh) + dot(ah, bl)


def kernel(
    e_in, h_in, p_in, j_in, w_in, g_in, r_in, lvl,
    out_e, out_f,
    eb, hb, jb, pb, wb, gb, rb, pump,
    hs, rxe, rxh, rye, ryh, rce, rch, sl, sr,
    gat, tab_h, tab_l, xt_h, xt_l, inn, sbuf, rbuf,
    load_sem, xe_s, xe_r, xh_s, xh_r, l1_s, l2_s, r1_s, r2_s,
    ye_r, yh_r, ce_r, ch_r, g_s, g_r, rs_s, rs_r, out_sem,
):
    gx = lax.axis_index("gx")
    gy = lax.axis_index("gy")
    y_lo = gx // 16
    xc = (gx // 4) % 4
    zc = gx % 4
    left, right = (gx + 31) % 32, (gx + 1) % 32
    down, up = (gy + 3) % 4, (gy + 1) % 4
    has_l, has_r = gx > 0, gx < 31
    has_d, has_u = gy > 0, gy < 3
    dest = y_lo * 4 + zc

    def gather_peers():
        for dx in range(4):
            for dy in range(4):
                if dx or dy:
                    px = y_lo * 16 + ((xc + dx) % 4) * 4 + zc
                    yield (px, (gy + dy) % 4)

    def scatter_peers():
        for d in range(1, 8):
            to = (dest + d) % 8
            yield to, ((to // 4) * 16 + xc * 4 + to % 4, gy)

    loads = [
        pltpu.make_async_copy(e_in, eb.at[0, :, :, pl.ds(0, NZ), :], load_sem.at[0]),
        pltpu.make_async_copy(h_in, hb.at[:, :, pl.ds(8, NZ), :], load_sem.at[1]),
        pltpu.make_async_copy(j_in, jb, load_sem.at[2]),
        pltpu.make_async_copy(p_in, pb, load_sem.at[3]),
        pltpu.make_async_copy(w_in, wb, load_sem.at[4]),
        pltpu.make_async_copy(g_in, gb, load_sem.at[5]),
        pltpu.make_async_copy(r_in, rb, load_sem.at[6]),
    ]
    for copy in loads:
        copy.start()

    barrier = pltpu.get_barrier_semaphore()

    def greet(device):
        pl.semaphore_signal(barrier, inc=1, device_id=device, device_id_type=MESH)

    for peer in gather_peers():
        greet(peer)
    for _, peer in scatter_peers():
        greet(peer)
    pl.when(has_l)(lambda: greet((left, gy)))
    pl.when(has_r)(lambda: greet((right, gy)))
    pl.when(has_l & has_u)(lambda: greet((left, up)))
    pl.when(has_r & has_d)(lambda: greet((right, down)))

    zero_row = jnp.zeros((8, LANES), F32)
    for c in range(3):
        for x in range(LX):
            eb[0, c, x, NZ:, :] = zero_row
            eb[1, c, x, NZ:, :] = zero_row
            hb[c, x, 0:8, :] = zero_row

    @pl.when(jnp.logical_not(has_r))
    def _():
        rxe[...] = jnp.zeros(rxe.shape, F32)

    @pl.when(jnp.logical_not(has_l))
    def _():
        rxh[...] = jnp.zeros(rxh.shape, F32)

    @pl.when(jnp.logical_not(has_u))
    def _():
        rye[...] = jnp.zeros(rye.shape, F32)

    @pl.when(jnp.logical_not(has_d))
    def _():
        ryh[...] = jnp.zeros(ryh.shape, F32)

    @pl.when(jnp.logical_not(has_l & has_u))
    def _():
        rce[...] = jnp.zeros(rce.shape, F32)

    @pl.when(jnp.logical_not(has_r & has_d))
    def _():
        rch[...] = jnp.zeros(rch.shape, F32)

    greeted = (
        22
        + has_l.astype(jnp.int32)
        + has_r.astype(jnp.int32)
        + (has_l & has_u).astype(jnp.int32)
        + (has_r & has_d).astype(jnp.int32)
    )
    pl.semaphore_wait(barrier, greeted)

    keep_l = has_l.astype(F32)
    keep_d = has_d.astype(F32)
    lane = lax.broadcasted_iota(jnp.int32, (CH, LANES), 1)
    first_lane = lane == 0
    last_lane = lane == LANES - 1

    def remote(src, dst, send, recv, device):
        return pltpu.make_async_remote_copy(
            src_ref=src, dst_ref=dst, send_sem=send, recv_sem=recv,
            device_id=device, device_id_type=MESH,
        )

    def xe_copy(s, par):
        return remote(eb.at[par, pl.ds(1, 2), 0, pl.ds(0, NZ), :], rxe.at[s], xe_s.at[s], xe_r.at[s], (left, gy))

    def xh_copy(s):
        return remote(hs.at[s], rxh.at[s], xh_s.at[s], xh_r.at[s], (right, gy))

    def l1_copy(s):
        return remote(sl.at[s], rye.at[s], l1_s.at[s], ye_r.at[s], (gx, down))

    def l2_copy(s):
        return remote(sl.at[s], rce.at[s], l2_s.at[s], ce_r.at[s], (right, down))

    def r1_copy(s):
        return remote(sr.at[s], ryh.at[s], r1_s.at[s], yh_r.at[s], (gx, up))

    def r2_copy(s):
        return remote(sr.at[s], rch.at[s], r2_s.at[s], ch_r.at[s], (left, up))

    def local_h(par, x, cut):
        z = pl.ds(cut * CH, CH)
        z1 = pl.ds(cut * CH + 1, CH)
        zh = pl.ds(8 + cut * CH, CH)
        ex, ey, ez = eb[par, 0, x, z, :], eb[par, 1, x, z, :], eb[par, 2, x, z, :]
        exz, eyz = eb[par, 0, x, z1, :], eb[par, 1, x, z1, :]
        exy = jnp.where(last_lane, 0.0, pltpu.roll(ex, LANES - 1, 1))
        ezy = jnp.where(last_lane, 0.0, pltpu.roll(ez, LANES - 1, 1))
        hx = hb[0, x, zh, :] - DT * ((ezy - ez) - (eyz - ey))
        if x < LX - 1:
            hy = hb[1, x, zh, :] - DT * ((exz - ex) - (eb[par, 2, x + 1, z, :] - ez))
            hz = hb[2, x, zh, :] - DT * ((eb[par, 1, x + 1, z, :] - ey) - (exy - ex))
        else:
            hy = hb[1, x, zh, :] - DT * ((exz - ex) + ez)
            hz = hb[2, x, zh, :] + DT * (ey + (exy - ex))
        return ex, ey, ez, hx, hy, hz

    def put(acc, value, at, to):
        return jnp.where(lane == to, jnp.broadcast_to(value[:, at : at + 1], (CH, LANES)), acc)

    def spread(ref, s, at):
        return jnp.broadcast_to(ref[s, :, at : at + 1], (CH, LANES))

    def e_pass(s, par, x):
        for cut in range(NCH):
            z = pl.ds(cut * CH, CH)
            zh = pl.ds(8 + cut * CH, CH)
            zb = pl.ds(7 + cut * CH, CH)
            ex, ey, ez = eb[par, 0, x, z, :], eb[par, 1, x, z, :], eb[par, 2, x, z, :]
            hx, hy, hz = hb[0, x, zh, :], hb[1, x, zh, :], hb[2, x, zh, :]
            if x == 0:
                hym = keep_l * (rxh[s, 0, z, :] + DT * ez)
                hzm = keep_l * (
                    rxh[s, 1, z, :] - DT * ey
                    + jnp.where(last_lane, DT * spread(rce, s, cut * 16 + 3), 0.0)
                )
            else:
                hym, hzm = hb[1, x - 1, zh, :], hb[2, x - 1, zh, :]
            edge_z = spread(ryh, s, cut * 16 + 4 + x) + DT * ex
            if x == LX - 1:
                edge_z = edge_z - DT * spread(rch, s, cut * 16 + 8)
            edge_x = spread(ryh, s, cut * 16 + x) - DT * ez
            dy_hz = hz - jnp.where(first_lane, keep_d * edge_z, pltpu.roll(hz, 1, 1))
            dy_hx = hx - jnp.where(first_lane, keep_d * edge_x, pltpu.roll(hx, 1, 1))
            curl_x = dy_hz - (hy - hb[1, x, zb, :])
            curl_y = (hx - hb[0, x, zb, :]) - (hz - hzm)
            curl_z = (hy - hym) - dy_hx
            inv = wb[x, z, :]
            gain = gb[x, z, :].astype(F32)
            drop = None
            for c, old, curl in ((0, ex, curl_x), (1, ey, curl_y), (2, ez, curl_z)):
                pol = pb[c, x, z, :]
                cur = gain * (C_J * jb[c, x, z, :] + C_D * (inv * old - pol))
                jb[c, x, z, :] = cur
                pb[c, x, z, :] = pol + DT * cur
                new = old + DT * (curl - cur)
                eb[1 - par, c, x, z, :] = new
                term = (old + new) * cur
                drop = term if drop is None else drop + term
            wb[x, z, :] = (1.0 - DT * REC) * inv + pump[x, z, :] - (0.5 * DT * SAT) * drop

    def wave_turns(col):
        f = gy * FL + col // LANES
        return (0.6 + 0.05 * f.astype(F32)) * (1.0 / (2.0 * math.pi))

    def direction(index):
        return 0.75 * (2.0 * index.astype(F32) - 63.0) / 63.0

    def build_tables():
        rows = 64

        def y_rows(i, carry):
            row = lax.broadcasted_iota(jnp.int32, (rows, LANES), 0) + i * rows
            col = lax.broadcasted_iota(jnp.int32, (rows, LANES), 1)
            base = (row.astype(F32) - 256.0) * direction(col % 64)
            quarter = jnp.where(col < 64, 0.25, 0.0)
            for f in range(FL):
                wave = (0.6 + 0.05 * (gy * FL + f).astype(F32)) * (1.0 / (2.0 * math.pi))
                high, low = split(sin_turns(wave * base + quarter))
                tab_h[pl.ds(i * rows, rows), f * LANES : (f + 1) * LANES] = high
                tab_l[pl.ds(i * rows, rows), f * LANES : (f + 1) * LANES] = low
            return carry

        lax.fori_loop(0, 512 // rows, y_rows, 0)
        row = lax.broadcasted_iota(jnp.int32, (64, LANES), 0)
        col = lax.broadcasted_iota(jnp.int32, (64, LANES), 1)
        to = row // 8
        a = 2 * ((to // 4) * 16 + xc * 4 + to % 4) + (row // 4) % 2
        cell = (y_lo * 16 + ((col % 64) // 16) * 4 + zc) * 4 + col % 4 - 64
        base = cell.astype(F32) * direction(a)
        quarter = jnp.where(col < 64, 0.25, 0.0)
        same = (row % 4) == ((col % 16) // 4)
        for f in range(FL):
            wave = (0.6 + 0.05 * (gy * FL + f).astype(F32)) * (1.0 / (2.0 * math.pi))
            value = jnp.where(same, sin_turns(wave * base + quarter), 0.0) * (1.0 / 256.0)
            high, low = split(value)
            xt_h[f] = high
            xt_l[f] = low
        inn[...] = jnp.zeros(inn.shape, F32)

    gather_bytes = pl.ds(0, 15)

    def gather_copies(n):
        mine = gat.at[n, gy * 4 + xc]
        return [remote(mine, mine, g_s.at[n], g_r.at[n], peer) for peer in gather_peers()]

    def gather_wait(n, sem):
        pltpu.make_async_copy(gat.at[n, gather_bytes], gat.at[n, gather_bytes], sem.at[n]).wait()

    def add_batch(n):
        gather_wait(n, g_r)
        lhs = jnp.concatenate(
            [gat[n, pl.ds(q * 4, 4)].reshape(64, LANES) for q in range(4)], axis=1
        )
        res = dot3(split(lhs), (tab_h[...], tab_l[...]))
        row = lax.broadcasted_iota(jnp.int32, (64, LANES), 0)
        col = lax.broadcasted_iota(jnp.int32, (64, LANES), 1)
        late = jnp.where((row % 16) < 8, 0.5, 1.0) + n.astype(F32)
        sign = jnp.where(col < 64, 1.0, -1.0)
        for f in range(FL):
            wave = (0.6 + 0.05 * (gy * FL + f).astype(F32)) * (1.0 / (2.0 * math.pi))
            turns = wave * DT * late
            part = res[:, f * LANES : (f + 1) * LANES]
            inn[:, f * LANES : (f + 1) * LANES] += DT * (
                sin_turns(turns + 0.25) * part + sin_turns(turns) * (sign * pltpu.roll(part, 64, 1))
            )

    loads[0].wait()
    pl.when(has_l)(lambda: xe_copy(0, 0).start())
    loads[1].wait()

    def step(s, carry):
        par = s % 2
        s = jnp.asarray(s, jnp.int32)
        pack_l = [jnp.zeros((CH, LANES), F32)]
        pack_r = [jnp.zeros((CH, LANES), F32)]

        def pack(cut, x, ex, ey, ez, hx, hz):
            pack_l[0] = put(pack_l[0], ex, 0, cut * 16 + x)
            pack_l[0] = put(pack_l[0], ez, 0, cut * 16 + 4 + x)
            pack_r[0] = put(pack_r[0], hx, LANES - 1, cut * 16 + x)
            pack_r[0] = put(pack_r[0], hz, LANES - 1, cut * 16 + 4 + x)
            if x == 0:
                pack_r[0] = put(pack_r[0], ey, LANES - 1, cut * 16 + 8)

        for x in (3, 0, 1, 2):
            for cut in range(NCH):
                zh = pl.ds(8 + cut * CH, CH)
                ex, ey, ez, hx, hy, hz = local_h(par, x, cut)
                hb[0, x, zh, :] = hx
                hb[1, x, zh, :] = hy
                hb[2, x, zh, :] = hz
                if x == 3:
                    z = pl.ds(cut * CH, CH)
                    hs[s, 0, z, :] = hy
                    hs[s, 1, z, :] = hz
                pack(cut, x, ex, ey, ez, hx, hz)
            if x == 3:
                pl.when(has_r)(lambda: xh_copy(s).start())
        sl[s] = pack_l[0]
        sr[s] = pack_r[0]
        pl.when(has_d)(lambda: l1_copy(s).start())
        pl.when(has_r & has_d)(lambda: l2_copy(s).start())
        pl.when(has_u)(lambda: r1_copy(s).start())
        pl.when(has_l & has_u)(lambda: r2_copy(s).start())

        @pl.when(s == 0)
        def _():
            for copy in loads[2:]:
                copy.wait()
            for x in range(LX):
                for cut in range(NCH):
                    z = pl.ds(cut * CH, CH)
                    region = rb[x, z, :]
                    rate = jnp.zeros((CH, LANES), F32)
                    for k in range(8):
                        rate = jnp.where(region == k, lvl[k], rate)
                    pump[x, z, :] = (DT * REC) * rate
            build_tables()

        @pl.when(s > 0)
        def _():
            add_batch(s - 1)

        pl.when(has_u)(lambda: l1_copy(s).wait_recv())
        pl.when(has_d)(lambda: r1_copy(s).wait_recv())
        pl.when(has_r & has_d)(lambda: r2_copy(s).wait_recv())
        for x in range(LX):
            for cut in range(NCH):
                zh = pl.ds(8 + cut * CH, CH)
                hb[0, x, zh, :] = hb[0, x, zh, :] - jnp.where(last_lane, DT * spread(rye, s, cut * 16 + 4 + x), 0.0)
                hb[2, x, zh, :] = hb[2, x, zh, :] + jnp.where(last_lane, DT * spread(rye, s, cut * 16 + x), 0.0)
        e_pass(s, par, 1)
        e_pass(s, par, 2)

        pl.when(has_l & has_u)(lambda: l2_copy(s).wait_recv())
        pl.when(has_l)(lambda: xh_copy(s).wait_recv())
        e_pass(s, par, 0)

        @pl.when((s < STEPS - 1) & has_l)
        def _():
            xe_copy(s + 1, 1 - par).start()

        pl.when(has_r)(lambda: xe_copy(s, par).wait_recv())
        for cut in range(NCH):
            z = pl.ds(cut * CH, CH)
            zh = pl.ds(8 + cut * CH, CH)
            hb[1, 3, zh, :] = hb[1, 3, zh, :] + DT * rxe[s, 1, z, :]
            hb[2, 3, zh, :] = hb[2, 3, zh, :] - DT * rxe[s, 0, z, :]
        e_pass(s, par, 3)

        me = gy * 4 + xc
        for x in range(LX):
            gat[s, me, pl.ds(x, 1), :] = -hb[1, x, pl.ds(8 + NZ - 1, 1), :]
            gat[s, me, pl.ds(4 + x, 1), :] = hb[0, x, pl.ds(8 + NZ - 1, 1), :]
            gat[s, me, pl.ds(8 + x, 1), :] = eb[1 - par, 1, x, pl.ds(NZ - 1, 1), :]
            gat[s, me, pl.ds(12 + x, 1), :] = -eb[1 - par, 0, x, pl.ds(NZ - 1, 1), :]
        for copy in gather_copies(s):
            copy.start()

        pl.when(has_l)(lambda: xe_copy(s, par).wait_send())
        pl.when(has_r)(lambda: xh_copy(s).wait_send())
        pl.when(has_d)(lambda: l1_copy(s).wait_send())
        pl.when(has_r & has_d)(lambda: l2_copy(s).wait_send())
        pl.when(has_u)(lambda: r1_copy(s).wait_send())
        pl.when(has_l & has_u)(lambda: r2_copy(s).wait_send())
        return carry

    lax.fori_loop(0, STEPS, step, 0)

    final = pltpu.make_async_copy(eb.at[0, :, :, pl.ds(0, NZ), :], out_e, out_sem)
    final.start()
    add_batch(jnp.int32(STEPS - 1))

    col = lax.broadcasted_iota(jnp.int32, (64, LANES), 1)
    sign = jnp.where(col < 64, -1.0, 1.0)
    for f in range(FL):
        part = inn[:, f * LANES : (f + 1) * LANES]
        rhs = jnp.concatenate([part, sign * pltpu.roll(part, 64, 1)], axis=0)
        res = dot3((xt_h[f], xt_l[f]), split(rhs))
        for d in range(8):
            sbuf[d, f] = res[8 * d : 8 * d + 8, :]

    scatter = [
        remote(sbuf.at[to], rbuf.at[dest], rs_s, rs_r, peer) for to, peer in scatter_peers()
    ]
    for copy in scatter:
        copy.start()
    rbuf[dest] = sbuf[dest]
    seven = pl.ds(0, 7)
    pltpu.make_async_copy(rbuf.at[seven], rbuf.at[seven], rs_r).wait()

    low_half = lax.broadcasted_iota(jnp.int32, (1, LANES), 1) < 64
    for f in range(FL):
        total = rbuf[0, f]
        for d in range(1, 8):
            total = total + rbuf[d, f]
        turned = pltpu.roll(total, 64, 1)
        for a in range(2):
            for pair in range(2):
                r0, r1 = a * 4 + 2 * pair, a * 4 + 2 * pair + 1
                real = jnp.where(low_half, total[r0 : r0 + 1, :], turned[r1 : r1 + 1, :])
                imag = jnp.where(low_half, turned[r0 : r0 + 1, :], total[r1 : r1 + 1, :])
                out_f[a, f : f + 1, pair * LANES : (pair + 1) * LANES] = real
                out_f[a, f : f + 1, 256 + pair * LANES : 256 + (pair + 1) * LANES] = imag

    pltpu.make_async_copy(sbuf.at[seven], sbuf.at[seven], rs_s).wait()

    def settle(n, carry):
        gather_wait(n, g_s)
        return carry

    lax.fori_loop(0, STEPS, settle, 0)
    final.wait()


def local(electric, magnetic, polarization, current, inversion, gain_mask, pump_region, pump_level):
    anywhere = pl.BlockSpec(memory_space=pl.ANY)
    dma = pltpu.SemaphoreType.DMA
    vmem = pltpu.VMEM
    state = (3, LX, NZ, LANES)
    return pl.pallas_call(
        kernel,
        out_shape=(
            jax.ShapeDtypeStruct(state, F32),
            jax.ShapeDtypeStruct((2, FL, 512), F32),
        ),
        in_specs=[anywhere] * 7 + [pl.BlockSpec(memory_space=pltpu.SMEM)],
        out_specs=(anywhere, pl.BlockSpec(memory_space=pltpu.VMEM)),
        scratch_shapes=[
            vmem((2, 3, LX, NZ + 8, LANES), F32),
            vmem((3, LX, NZ + 8, LANES), F32),
            vmem(state, F32),
            vmem(state, F32),
            vmem(state[1:], F32),
            vmem(state[1:], jnp.int32),
            vmem(state[1:], jnp.int32),
            vmem(state[1:], F32),
            vmem((STEPS, 2, NZ, LANES), F32),
            vmem((STEPS, 2, NZ, LANES), F32),
            vmem((STEPS, 2, NZ, LANES), F32),
            vmem((STEPS, CH, LANES), F32),
            vmem((STEPS, CH, LANES), F32),
            vmem((STEPS, CH, LANES), F32),
            vmem((STEPS, CH, LANES), F32),
            vmem((STEPS, CH, LANES), F32),
            vmem((STEPS, CH, LANES), F32),
            vmem((STEPS, 16, 16, LANES), F32),
            vmem((512, FL * LANES), BF16),
            vmem((512, FL * LANES), BF16),
            vmem((FL, 64, LANES), BF16),
            vmem((FL, 64, LANES), BF16),
            vmem((64, FL * LANES), F32),
            vmem((8, FL, 8, LANES), F32),
            vmem((8, FL, 8, LANES), F32),
            dma((7,)),
        ]
        + [dma((STEPS,))] * 14
        + [dma, dma, dma],
        compiler_params=pltpu.CompilerParams(
            collective_id=0, has_side_effects=True, vmem_limit_bytes=48 << 20
        ),
    )(electric, magnetic, polarization, current, inversion, gain_mask, pump_region, pump_level)


def solution(mesh):
    return jax.shard_map(
        local,
        mesh=mesh,
        in_specs=(
            P(None, "gx", None, "gy"),
            P(None, "gx", None, "gy"),
            P(None, "gx", None, "gy"),
            P(None, "gx", None, "gy"),
            P("gx", None, "gy"),
            P("gx", None, "gy"),
            P("gx", None, "gy"),
            P(),
        ),
        out_specs=(P(None, "gx", None, "gy"), P("gx", "gy", None)),
        check_vma=False,
    )
```

```python
import functools
import math

import jax
import jax.numpy as jnp
from jax import lax
from jax.experimental import pallas as pl
from jax.experimental.pallas import tpu as pltpu
from jax.sharding import PartitionSpec as P

MESH = pl.DeviceIdType.MESH
F32 = jnp.float32
BF16 = jnp.bfloat16

STEPS = 4
NZ = 96
LX = 4
LANES = 128
CH = 32
NCH = NZ // CH
FL = 4

DT = 0.5
DAMP = 0.4
SAT = 0.5
REC = 0.8
SCALE = DT * DT / (1.0 + 0.5 * DAMP * DT)
KEEP = (1.0 - 0.5 * DAMP * DT) / (DT * DT)


def sin_turns(turns):
    r = turns - jnp.floor(turns + 0.5)
    x = r * (2.0 * math.pi)
    s = x * x
    acc = jnp.full_like(s, 1.0 / math.factorial(17))
    for order, sign in ((15, -1.0), (13, 1.0), (11, -1.0), (9, 1.0), (7, -1.0), (5, 1.0), (3, -1.0), (1, 1.0)):
        acc = acc * s + sign / math.factorial(order)
    return acc * x


def split(value):
    high = value.astype(BF16)
    return high, (value - high.astype(F32)).astype(BF16)


def dot3(a, b):
    ah, al = a
    bh, bl = b
    dot = functools.partial(jnp.dot, preferred_element_type=F32)
    return dot(ah, bh) + dot(al, bh) + dot(ah, bl)


def kernel(
    e_in, h_in, p_in, j_in, w_in, g_in, r_in, lvl_in,
    out_e, out_f,
    eb, hb, jb, pb, wb, gi, gb, rb, pump,
    hs, rxe, rxh, rye, ryh, rce, rch, sl, sr, tl, tr,
    gat, tab_h, tab_l, xt_h, xt_l, inn, sbuf, rbuf,
    lvl, load_sem, xe_s, xe_r, xh_s, xh_r, l1_s, l2_s, r1_s, r2_s,
    ye_r, yh_r, ce_r, ch_r, g_s, g_r, rs_s, rs_r, out_sem,
):
    gx = lax.axis_index("gx")
    gy = lax.axis_index("gy")
    y_lo = gx // 16
    xc = (gx // 4) % 4
    zc = gx % 4
    left, right = (gx + 31) % 32, (gx + 1) % 32
    down, up = (gy + 3) % 4, (gy + 1) % 4
    has_l, has_r = gx > 0, gx < 31
    has_d, has_u = gy > 0, gy < 3
    dest = y_lo * 4 + zc

    def gather_peers():
        for dx in range(4):
            for dy in range(4):
                if dx or dy:
                    px = y_lo * 16 + ((xc + dx) % 4) * 4 + zc
                    yield (px, (gy + dy) % 4)

    def scatter_peers():
        for d in range(1, 8):
            to = (dest + d) % 8
            yield to, ((to // 4) * 16 + xc * 4 + to % 4, gy)

    def load(src, dst, index):
        return pltpu.make_async_copy(src, dst, load_sem.at[index])

    body, body_h = pl.ds(0, NZ), pl.ds(8, NZ)
    inner, outer = pl.ds(0, LX - 1), pl.ds(LX - 1, 1)
    loads = [
        load(e_in.at[:, outer], eb.at[0, :, outer, body, :], 0),
        load(h_in.at[:, outer], hb.at[:, outer, body_h, :], 1),
        load(e_in.at[:, inner], eb.at[0, :, inner, body, :], 2),
        load(h_in.at[:, inner], hb.at[:, inner, body_h, :], 3),
        load(j_in, jb, 4),
        load(p_in, pb, 5),
        load(w_in, wb, 6),
        load(g_in, gi, 7),
        load(r_in, rb, 8),
        load(lvl_in, lvl, 9),
    ]
    for copy in loads:
        copy.start()

    barrier = pltpu.get_barrier_semaphore()

    def greet(device):
        pl.semaphore_signal(barrier, inc=1, device_id=device, device_id_type=MESH)

    pl.when(has_l)(lambda: greet((left, gy)))
    pl.when(has_r)(lambda: greet((right, gy)))
    pl.when(has_l & has_u)(lambda: greet((left, up)))
    pl.when(has_r & has_d)(lambda: greet((right, down)))
    for peer in gather_peers():
        greet(peer)
    for _, peer in scatter_peers():
        greet(peer)

    zero_row = jnp.zeros((8, LANES), F32)
    for c in range(3):
        for x in range(LX):
            eb[0, c, x, NZ:, :] = zero_row
            eb[1, c, x, NZ:, :] = zero_row
            hb[c, x, 0:8, :] = zero_row
    for step in range(STEPS):
        rxe[step, 1, 0:8, :] = zero_row

    @pl.when(jnp.logical_not(has_r))
    def _():
        rxe[...] = jnp.zeros(rxe.shape, F32)

    @pl.when(jnp.logical_not(has_l))
    def _():
        rxh[...] = jnp.zeros(rxh.shape, F32)

    @pl.when(jnp.logical_not(has_u))
    def _():
        rye[...] = jnp.zeros(rye.shape, F32)

    @pl.when(jnp.logical_not(has_d))
    def _():
        ryh[...] = jnp.zeros(ryh.shape, F32)

    @pl.when(jnp.logical_not(has_l & has_u))
    def _():
        rce[...] = jnp.zeros(rce.shape, F32)

    @pl.when(jnp.logical_not(has_r & has_d))
    def _():
        rch[...] = jnp.zeros(rch.shape, F32)

    edge_l = has_l.astype(F32) * DT
    edge_d = has_d.astype(F32) * DT
    lane = lax.broadcasted_iota(jnp.int32, (CH, LANES), 1)
    first_lane = lane == 0
    last_lane = lane == LANES - 1

    def remote(src, dst, send, recv, device):
        return pltpu.make_async_remote_copy(
            src_ref=src, dst_ref=dst, send_sem=send, recv_sem=recv,
            device_id=device, device_id_type=MESH,
        )

    def xe_copy(s, par, cut):
        z, zr = pl.ds(cut * CH, CH), pl.ds(8 + cut * CH, CH)
        return remote(
            eb.at[par, pl.ds(1, 2), 0, z, :], rxe.at[s, :, zr, :],
            xe_s.at[s], xe_r.at[s * NCH + cut], (left, gy),
        )

    def xh_copy(s, cut):
        z = pl.ds(cut * CH, CH)
        return remote(
            hs.at[s, :, z, :], rxh.at[s, :, z, :],
            xh_s.at[s], xh_r.at[s * NCH + cut], (right, gy),
        )

    def l1_copy(s):
        return remote(sl.at[s], rye.at[s], l1_s.at[s], ye_r.at[s], (gx, down))

    def l2_copy(s):
        return remote(tl.at[s], rce.at[s], l2_s.at[s], ce_r.at[s], (right, down))

    def r1_copy(s):
        return remote(sr.at[s], ryh.at[s], r1_s.at[s], yh_r.at[s], (gx, up))

    def r2_copy(s):
        return remote(tr.at[s], rch.at[s], r2_s.at[s], ch_r.at[s], (left, up))

    def local_h(par, x, cut):
        z = pl.ds(cut * CH, CH)
        z1 = pl.ds(cut * CH + 1, CH)
        zh = pl.ds(8 + cut * CH, CH)
        ex, ey, ez = eb[par, 0, x, z, :], eb[par, 1, x, z, :], eb[par, 2, x, z, :]
        exz, eyz = eb[par, 0, x, z1, :], eb[par, 1, x, z1, :]
        exy = jnp.where(last_lane, 0.0, pltpu.roll(ex, LANES - 1, 1))
        ezy = jnp.where(last_lane, 0.0, pltpu.roll(ez, LANES - 1, 1))
        hx = hb[0, x, zh, :] - DT * ((ezy - ez) - (eyz - ey))
        if x < LX - 1:
            hy = hb[1, x, zh, :] - DT * ((exz - ex) - (eb[par, 2, x + 1, z, :] - ez))
            hz = hb[2, x, zh, :] - DT * ((eb[par, 1, x + 1, z, :] - ey) - (exy - ex))
        else:
            hy = hb[1, x, zh, :] - DT * ((exz - ex) + ez)
            hz = hb[2, x, zh, :] + DT * (ey + (exy - ex))
        hb[0, x, zh, :] = hx
        hb[1, x, zh, :] = hy
        hb[2, x, zh, :] = hz
        if x == LX - 1:
            return hy, hz
        return hx, hz

    def outer_h(s, par, cut):
        z = pl.ds(cut * CH, CH)
        hs[s, 0, z, :], hs[s, 1, z, :] = local_h(par, LX - 1, cut)

    def turn(value, at, to):
        shift = (to - at) % LANES
        return pltpu.roll(value, shift, 1) if shift else value

    def put(acc, value, at, to):
        return jnp.where(lane == to, turn(value, at, to), acc)

    def drop_rate(x, z, drop):
        wb[x, z, :] = (1.0 - DT * REC) * wb[x, z, :] + pump[x, z, :] - (0.5 * SAT) * drop

    def e_pass(par, x, keep):
        for cut in range(NCH):
            z = pl.ds(cut * CH, CH)
            zh = pl.ds(8 + cut * CH, CH)
            zb = pl.ds(7 + cut * CH, CH)
            ex, ey, ez = eb[par, 0, x, z, :], eb[par, 1, x, z, :], eb[par, 2, x, z, :]
            hx, hy, hz = hb[0, x, zh, :], hb[1, x, zh, :], hb[2, x, zh, :]
            dy_hz = hz - jnp.where(first_lane, edge_d * ex, pltpu.roll(hz, 1, 1))
            dy_hx = hx + jnp.where(first_lane, edge_d * ez, -pltpu.roll(hx, 1, 1))
            if x == 0:
                dx_hz = hz + edge_l * ey
                dx_hy = hy - edge_l * ez
            else:
                dx_hz = hz - hb[2, x - 1, zh, :]
                dx_hy = hy - hb[1, x - 1, zh, :]
            curl_x = dy_hz - (hy - hb[1, x, zb, :])
            curl_y = (hx - hb[0, x, zb, :]) - dx_hz
            curl_z = dx_hy - dy_hx
            inv = wb[x, z, :]
            gain = gb[x, z, :]
            for c, old, curl in ((0, ex, curl_x), (1, ey, curl_y), (2, ez, curl_z)):
                pol = pb[c, x, z, :]
                cur = gain * (keep * jb[c, x, z, :] + (inv * old - pol))
                jb[c, x, z, :] = cur
                pb[c, x, z, :] = pol + cur
                eb[1 - par, c, x, z, :] = old + (DT * curl - cur)

    small_lane = lane % 16
    top_row = lax.broadcasted_iota(jnp.int32, (CH, LANES), 0) == 0
    edge_lanes = first_lane | last_lane

    def fix_y(s, par):
        ye, yh = rye[s], ryh[s]
        ye8, yh8 = pltpu.roll(ye, LANES - 8, 1), pltpu.roll(yh, LANES - 8, 1)
        under = pltpu.roll(ye8, 1, 0)
        under = jnp.where(top_row, jnp.where(lane < 16, 0.0, pltpu.roll(under, 16, 1)), under)
        before = jnp.where(small_lane >= 2, pltpu.roll(ye, 2, 1), 0.0)
        add_x = (DT * DT) * ye - DT * yh8
        add_y = (DT * DT) * ((before - ye) - (ye8 - under))
        add_z = (DT * DT) * ye8 + DT * yh
        new = 1 - par
        for x in (0, 3, 1, 2):
            for cut in range(NCH):
                z = pl.ds(cut * CH, CH)
                zh = pl.ds(8 + cut * CH, CH)
                at = cut * 16 + 2 * x
                eb[new, 0, x, z, :] = eb[new, 0, x, z, :] + jnp.where(edge_lanes, turn(add_x, at, LANES - 1), 0.0)
                eb[new, 1, x, z, :] = eb[new, 1, x, z, :] + jnp.where(last_lane, turn(add_y, at, LANES - 1), 0.0)
                eb[new, 2, x, z, :] = eb[new, 2, x, z, :] + jnp.where(edge_lanes, turn(add_z, at, LANES - 1), 0.0)
                hb[0, x, zh, :] = hb[0, x, zh, :] - jnp.where(last_lane, DT * turn(ye8, at, LANES - 1), 0.0)
                hb[2, x, zh, :] = hb[2, x, zh, :] + jnp.where(last_lane, DT * turn(ye, at, LANES - 1), 0.0)

    def late_inversion(par, x):
        for cut in range(NCH):
            z = pl.ds(cut * CH, CH)
            drop = None
            for c in range(3):
                term = (eb[par, c, x, z, :] + eb[1 - par, c, x, z, :]) * jb[c, x, z, :]
                drop = term if drop is None else drop + term
            drop_rate(x, z, drop)

    def fix_first(s, par, cut):
        z = pl.ds(cut * CH, CH)
        corner = jnp.where(last_lane, (DT * DT) * turn(rce[s], cut * 16, LANES - 1), 0.0)
        eb[1 - par, 1, 0, z, :] = eb[1 - par, 1, 0, z, :] + (DT * rxh[s, 1, z, :] + corner)
        eb[1 - par, 2, 0, z, :] = eb[1 - par, 2, 0, z, :] - DT * rxh[s, 0, z, :]

    def fix_outer(s, par, cut):
        x = LX - 1
        z = pl.ds(cut * CH, CH)
        zh = pl.ds(8 + cut * CH, CH)
        zb = pl.ds(7 + cut * CH, CH)
        ry = DT * rxe[s, 1, zh, :]
        rz = DT * rxe[s, 0, zh, :]
        hb[1, x, zh, :] = hb[1, x, zh, :] + ry
        hb[2, x, zh, :] = hb[2, x, zh, :] - rz
        side = jnp.where(first_lane, DT * turn(rch[s], cut * 16, 0), pltpu.roll(rz, 1, 1))
        back = DT * rxe[s, 1, zb, :]
        eb[1 - par, 0, x, z, :] = eb[1 - par, 0, x, z, :] + DT * ((side - rz) - (ry - back))
        eb[1 - par, 1, x, z, :] = eb[1 - par, 1, x, z, :] + DT * rz
        eb[1 - par, 2, x, z, :] = eb[1 - par, 2, x, z, :] + DT * ry

    def wave_turns(col):
        f = gy * FL + col // LANES
        return (0.6 + 0.05 * f.astype(F32)) * (1.0 / (2.0 * math.pi))

    def direction(index):
        return 0.75 * (2.0 * index.astype(F32) - 63.0) / 63.0

    def build_tables():
        rows = 64

        def y_rows(i, carry):
            row = lax.broadcasted_iota(jnp.int32, (rows, LANES), 0) + i * rows
            col = lax.broadcasted_iota(jnp.int32, (rows, LANES), 1)
            base = (row.astype(F32) - 256.0) * direction(col % 64)
            quarter = jnp.where(col < 64, 0.25, 0.0)
            for f in range(FL):
                wave = (0.6 + 0.05 * (gy * FL + f).astype(F32)) * (1.0 / (2.0 * math.pi))
                high, low = split(sin_turns(wave * base + quarter))
                tab_h[pl.ds(i * rows, rows), f * LANES : (f + 1) * LANES] = high
                tab_l[pl.ds(i * rows, rows), f * LANES : (f + 1) * LANES] = low
            return carry

        lax.fori_loop(0, 512 // rows, y_rows, 0)
        row = lax.broadcasted_iota(jnp.int32, (64, LANES), 0)
        col = lax.broadcasted_iota(jnp.int32, (64, LANES), 1)
        to = row // 8
        a = 2 * ((to // 4) * 16 + xc * 4 + to % 4) + (row // 4) % 2
        cell = (y_lo * 16 + ((col % 64) // 16) * 4 + zc) * 4 + col % 4 - 64
        base = cell.astype(F32) * direction(a)
        quarter = jnp.where(col < 64, 0.25, 0.0)
        same = (row % 4) == ((col % 16) // 4)
        for f in range(FL):
            wave = (0.6 + 0.05 * (gy * FL + f).astype(F32)) * (1.0 / (2.0 * math.pi))
            value = jnp.where(same, sin_turns(wave * base + quarter), 0.0) * (1.0 / 256.0)
            high, low = split(value)
            xt_h[f] = high
            xt_l[f] = low
        inn[...] = jnp.zeros(inn.shape, F32)

    gather_bytes = pl.ds(0, 15)

    def gather_copies(n):
        mine = gat.at[n, gy * 4 + xc]
        return [remote(mine, mine, g_s.at[n], g_r.at[n], peer) for peer in gather_peers()]

    def gather_wait(n, sem):
        pltpu.make_async_copy(gat.at[n, gather_bytes], gat.at[n, gather_bytes], sem.at[n]).wait()

    def add_batch(n):
        gather_wait(n, g_r)
        lhs = jnp.concatenate(
            [gat[n, pl.ds(q * 4, 4)].reshape(64, LANES) for q in range(4)], axis=1
        )
        res = dot3(split(lhs), (tab_h[...], tab_l[...]))
        row = lax.broadcasted_iota(jnp.int32, (64, LANES), 0)
        col = lax.broadcasted_iota(jnp.int32, (64, LANES), 1)
        late = jnp.where((row % 16) < 8, 0.5, 1.0) + n.astype(F32)
        sign = jnp.where(col < 64, 1.0, -1.0)
        for f in range(FL):
            wave = (0.6 + 0.05 * (gy * FL + f).astype(F32)) * (1.0 / (2.0 * math.pi))
            turns = wave * DT * late
            part = res[:, f * LANES : (f + 1) * LANES]
            inn[:, f * LANES : (f + 1) * LANES] += DT * (
                sin_turns(turns + 0.25) * part + sin_turns(turns) * (sign * pltpu.roll(part, 64, 1))
            )

    loads[0].wait()
    loads[1].wait()
    for cut in range(NCH - 1, -1, -1):
        outer_h(0, 0, cut)
    loads[2].wait()
    greeted = (
        22
        + has_l.astype(jnp.int32)
        + has_r.astype(jnp.int32)
        + (has_l & has_u).astype(jnp.int32)
        + (has_r & has_d).astype(jnp.int32)
    )
    pl.semaphore_wait(barrier, greeted)

    @pl.when(has_l)
    def _():
        for cut in range(NCH - 1, -1, -1):
            xe_copy(0, 0, cut).start()

    @pl.when(has_r)
    def _():
        for cut in range(NCH - 1, -1, -1):
            xh_copy(0, cut).start()

    def send_corners(s, par):
        left_col = jnp.zeros((CH, LANES), F32)
        right_col = jnp.zeros((CH, LANES), F32)
        for cut in range(NCH):
            z = pl.ds(cut * CH, CH)
            left_col = put(left_col, eb[par, 0, LX - 1, z, :], 0, cut * 16)
            right_col = put(right_col, eb[par, 1, 0, z, :], LANES - 1, cut * 16)
        tl[s] = left_col
        tr[s] = right_col
        pl.when(has_r & has_d)(lambda: l2_copy(s).start())
        pl.when(has_l & has_u)(lambda: r2_copy(s).start())

    def send_low(s, par):
        pack = jnp.zeros((CH, LANES), F32)
        for x in range(LX):
            for cut in range(NCH):
                z = pl.ds(cut * CH, CH)
                pack = put(pack, eb[par, 0, x, z, :], 0, cut * 16 + 2 * x)
                pack = put(pack, eb[par, 2, x, z, :], 0, cut * 16 + 8 + 2 * x)
        sl[s] = pack
        pl.when(has_d)(lambda: l1_copy(s).start())

    send_corners(0, 0)
    loads[3].wait()

    def show_plane(s, par):
        me = gy * 4 + xc
        for x in range(LX):
            gat[s, me, pl.ds(x, 1), :] = -hb[1, x, pl.ds(8 + NZ - 1, 1), :]
            gat[s, me, pl.ds(4 + x, 1), :] = hb[0, x, pl.ds(8 + NZ - 1, 1), :]
            gat[s, me, pl.ds(8 + x, 1), :] = eb[1 - par, 1, x, pl.ds(NZ - 1, 1), :]
            gat[s, me, pl.ds(12 + x, 1), :] = -eb[1 - par, 0, x, pl.ds(NZ - 1, 1), :]

    def gather_start(s):
        for copy in gather_copies(s):
            copy.start()

    def step(s, carry):
        s = jnp.asarray(s, jnp.int32)
        par = s % 2
        more = s < STEPS - 1
        send_low(s, par)
        pack = jnp.zeros((CH, LANES), F32)
        for x in (3, 0, 1, 2):
            for cut in range(NCH):
                if x < LX - 1:
                    hx, hz = local_h(par, x, cut)
                else:
                    zh = pl.ds(8 + cut * CH, CH)
                    hx, hz = hb[0, x, zh, :], hb[2, x, zh, :]
                pack = put(pack, hx, LANES - 1, cut * 16 + 2 * x + 1)
                pack = put(pack, hz, LANES - 1, cut * 16 + 8 + 2 * x + 1)
        sr[s] = pack
        pl.when(has_u)(lambda: r1_copy(s).start())

        @pl.when(s == 0)
        def _():
            for copy in loads[4:]:
                copy.wait()
            for x in range(LX):
                for cut in range(NCH):
                    z = pl.ds(cut * CH, CH)
                    region = rb[x, z, :]
                    rate = jnp.zeros((CH, LANES), F32)
                    for k in range(8):
                        rate = jnp.where(region == k, lvl[k], rate)
                    pump[x, z, :] = (DT * REC) * rate
                    gb[x, z, :] = SCALE * gi[x, z, :].astype(F32)

        @pl.when(s > 0)
        def _():
            for x in range(LX):
                late_inversion(par, x)
            gather_start(s - 1)

        keep = jnp.where(s == 0, KEEP * DT, KEEP)
        for x in (0, 3, 1, 2):
            e_pass(par, x, keep)
        pl.when(s == 1)(build_tables)
        pl.when(s > 1)(lambda: add_batch(s - 2))

        pl.when(has_u)(lambda: l1_copy(s).wait_recv())
        pl.when(has_d)(lambda: r1_copy(s).wait_recv())
        fix_y(s, par)

        pl.when(has_r & has_d)(lambda: r2_copy(s).wait_recv())
        pl.when(has_l & has_u)(lambda: l2_copy(s).wait_recv())

        def finish_outer(cut):
            fix_outer(s, par, cut)

            @pl.when(more)
            def _():
                outer_h(s + 1, 1 - par, cut)
                pl.when(has_r)(lambda: xh_copy(s + 1, cut).start())

        for cut in range(NCH - 1, -1, -1):
            pl.when(has_l)(lambda: xh_copy(s, cut).wait_recv())
            fix_first(s, par, cut)
            pl.when(more & has_l)(lambda: xe_copy(s + 1, 1 - par, cut).start())
            pl.when(has_r)(lambda: xe_copy(s, par, cut).wait_recv())
            if cut < NCH - 1:
                if cut == NCH - 2:
                    fix_outer(s, par, cut + 1)
                    show_plane(s, par)

                    @pl.when(more)
                    def _():
                        outer_h(s + 1, 1 - par, cut + 1)
                        pl.when(has_r)(lambda: xh_copy(s + 1, cut + 1).start())

                    pl.when(jnp.logical_not(more))(lambda: gather_start(s))
                else:
                    finish_outer(cut + 1)
        finish_outer(0)
        pl.when(more)(lambda: send_corners(s + 1, 1 - par))

        @pl.when(has_l)
        def _():
            whole = eb.at[par, pl.ds(1, 2), 0, body, :]
            remote(whole, rxe.at[s, :, body_h, :], xe_s.at[s], xe_r.at[0], (left, gy)).wait_send()

        @pl.when(has_r)
        def _():
            remote(hs.at[s], rxh.at[s], xh_s.at[s], xh_r.at[0], (right, gy)).wait_send()

        pl.when(has_d)(lambda: l1_copy(s).wait_send())
        pl.when(has_u)(lambda: r1_copy(s).wait_send())
        pl.when(has_r & has_d)(lambda: l2_copy(s).wait_send())
        pl.when(has_l & has_u)(lambda: r2_copy(s).wait_send())
        return carry

    lax.fori_loop(0, STEPS, step, 0)

    final = pltpu.make_async_copy(eb.at[0, :, :, body, :], out_e, out_sem)
    final.start()
    add_batch(jnp.int32(STEPS - 2))
    add_batch(jnp.int32(STEPS - 1))

    col = lax.broadcasted_iota(jnp.int32, (64, LANES), 1)
    sign = jnp.where(col < 64, -1.0, 1.0)
    for f in range(FL):
        part = inn[:, f * LANES : (f + 1) * LANES]
        rhs = jnp.concatenate([part, sign * pltpu.roll(part, 64, 1)], axis=0)
        res = dot3((xt_h[f], xt_l[f]), split(rhs))
        for d in range(8):
            sbuf[d, f] = res[8 * d : 8 * d + 8, :]

    scatter = [
        remote(sbuf.at[to], rbuf.at[dest], rs_s, rs_r, peer) for to, peer in scatter_peers()
    ]
    for copy in scatter:
        copy.start()
    rbuf[dest] = sbuf[dest]
    seven = pl.ds(0, 7)
    pltpu.make_async_copy(rbuf.at[seven], rbuf.at[seven], rs_r).wait()

    low_half = lax.broadcasted_iota(jnp.int32, (1, LANES), 1) < 64
    for f in range(FL):
        total = rbuf[0, f]
        for d in range(1, 8):
            total = total + rbuf[d, f]
        turned = pltpu.roll(total, 64, 1)
        for a in range(2):
            for pair in range(2):
                r0, r1 = a * 4 + 2 * pair, a * 4 + 2 * pair + 1
                real = jnp.where(low_half, total[r0 : r0 + 1, :], turned[r1 : r1 + 1, :])
                imag = jnp.where(low_half, turned[r0 : r0 + 1, :], total[r1 : r1 + 1, :])
                out_f[a, f : f + 1, pair * LANES : (pair + 1) * LANES] = real
                out_f[a, f : f + 1, 256 + pair * LANES : 256 + (pair + 1) * LANES] = imag

    pltpu.make_async_copy(sbuf.at[seven], sbuf.at[seven], rs_s).wait()

    def settle(n, carry):
        gather_wait(n, g_s)
        return carry

    lax.fori_loop(0, STEPS, settle, 0)
    final.wait()


def local(electric, magnetic, polarization, current, inversion, gain_mask, pump_region, pump_level):
    far_memory = pl.BlockSpec(memory_space=pltpu.HBM)
    near_memory = pl.BlockSpec(memory_space=pltpu.VMEM)
    dma = pltpu.SemaphoreType.DMA
    vmem = pltpu.VMEM
    state = (3, LX, NZ, LANES)
    operands = [
        pltpu.with_memory_space_constraint(operand, pltpu.HBM)
        for operand in (
            electric, magnetic, polarization, current, inversion, gain_mask, pump_region, pump_level,
        )
    ]
    return pl.pallas_call(
        kernel,
        out_shape=(
            jax.ShapeDtypeStruct(state, F32),
            jax.ShapeDtypeStruct((2, FL, 512), F32),
        ),
        in_specs=[far_memory] * 8,
        out_specs=(near_memory, near_memory),
        scratch_shapes=[
            vmem((2, 3, LX, NZ + 8, LANES), F32),
            vmem((3, LX, NZ + 8, LANES), F32),
            vmem(state, F32),
            vmem(state, F32),
            vmem(state[1:], F32),
            vmem(state[1:], jnp.int32),
            vmem(state[1:], F32),
            vmem(state[1:], jnp.int32),
            vmem(state[1:], F32),
            vmem((STEPS, 2, NZ, LANES), F32),
            vmem((STEPS, 2, NZ + 8, LANES), F32),
            vmem((STEPS, 2, NZ, LANES), F32),
            vmem((STEPS, CH, LANES), F32),
            vmem((STEPS, CH, LANES), F32),
            vmem((STEPS, CH, LANES), F32),
            vmem((STEPS, CH, LANES), F32),
            vmem((STEPS, CH, LANES), F32),
            vmem((STEPS, CH, LANES), F32),
            vmem((STEPS, CH, LANES), F32),
            vmem((STEPS, CH, LANES), F32),
            vmem((STEPS, 16, 16, LANES), F32),
            vmem((512, FL * LANES), BF16),
            vmem((512, FL * LANES), BF16),
            vmem((FL, 64, LANES), BF16),
            vmem((FL, 64, LANES), BF16),
            vmem((64, FL * LANES), F32),
            vmem((8, FL, 8, LANES), F32),
            vmem((8, FL, 8, LANES), F32),
            pltpu.SMEM((8,), F32),
            dma((10,)),
            dma((STEPS,)),
            dma((STEPS * NCH,)),
            dma((STEPS,)),
            dma((STEPS * NCH,)),
        ]
        + [dma((STEPS,))] * 10
        + [dma, dma, dma],
        compiler_params=pltpu.CompilerParams(
            collective_id=0, has_side_effects=True, vmem_limit_bytes=24 << 20
        ),
    )(*operands)


def solution(mesh):
    return jax.shard_map(
        local,
        mesh=mesh,
        in_specs=(
            P(None, "gx", None, "gy"),
            P(None, "gx", None, "gy"),
            P(None, "gx", None, "gy"),
            P(None, "gx", None, "gy"),
            P("gx", None, "gy"),
            P("gx", None, "gy"),
            P("gx", None, "gy"),
            P(),
        ),
        out_specs=(P(None, "gx", None, "gy"), P("gx", "gy", None)),
        check_vma=False,
    )
```

```python
import functools
import math

import jax
import jax.numpy as jnp
from jax import lax
from jax.experimental import pallas as pl
from jax.experimental.pallas import tpu as pltpu
from jax.sharding import PartitionSpec as P

MESH = pl.DeviceIdType.MESH
F32 = jnp.float32
BF16 = jnp.bfloat16

STEPS = 4
NZ = 96
LX = 4
LANES = 128
CH = 32
NCH = NZ // CH
FL = 4

DT = 0.5
DAMP = 0.4
SAT = 0.5
REC = 0.8
SCALE = DT * DT / (1.0 + 0.5 * DAMP * DT)
KEEP = (1.0 - 0.5 * DAMP * DT) / (DT * DT)


def sin_turns(turns):
    r = turns - jnp.floor(turns + 0.5)
    x = r * (2.0 * math.pi)
    s = x * x
    acc = jnp.full_like(s, 1.0 / math.factorial(17))
    for order, sign in ((15, -1.0), (13, 1.0), (11, -1.0), (9, 1.0), (7, -1.0), (5, 1.0), (3, -1.0), (1, 1.0)):
        acc = acc * s + sign / math.factorial(order)
    return acc * x


def split(value):
    high = value.astype(BF16)
    return high, (value - high.astype(F32)).astype(BF16)


def dot3(a, b):
    ah, al = a
    bh, bl = b
    dot = functools.partial(jnp.dot, preferred_element_type=F32)
    return dot(ah, bh) + dot(al, bh) + dot(ah, bl)


def kernel(
    e_in, h_in, p_in, j_in, w_in, g_in, r_in, lvl_in,
    out_e, out_f,
    eb, hb, jb, pb, wb, gi, gb, rb, pump,
    hs, rxe, rxh, rye, ryh, rce, rch, sl, sr, tl, tr,
    gat, gho, tab_h, tab_l, xt_h, xt_l, inn, sbuf, rbuf,
    lvl, load_sem, xe_s, xe_r, xh_s, xh_r, l1_s, l2_s, r1_s, r2_s,
    ye_r, yh_r, ce_r, ch_r, g_s, g_r, rs_s, rs_r, out_sem,
):
    gx = lax.axis_index("gx")
    gy = lax.axis_index("gy")
    y_lo = gx // 16
    xc = (gx // 4) % 4
    zc = gx % 4
    left, right = (gx + 31) % 32, (gx + 1) % 32
    down, up = (gy + 3) % 4, (gy + 1) % 4
    has_l, has_r = gx > 0, gx < 31
    has_d, has_u = gy > 0, gy < 3
    dest = xc * 4 + zc

    def gather_peers():
        for dl in range(2):
            for dy in range(4):
                if dl or dy:
                    yield ((gx + 16 * dl) % 32, (gy + dy) % 4)

    def scatter_peers():
        for d in range(1, 16):
            to = (dest + d) % 16
            yield to, (y_lo * 16 + to, gy)

    def load(src, dst, index):
        return pltpu.make_async_copy(src, dst, load_sem.at[index])

    body, body_h = pl.ds(0, NZ), pl.ds(8, NZ)
    inner, outer = pl.ds(0, LX - 1), pl.ds(LX - 1, 1)
    loads = [
        load(e_in.at[:, outer], eb.at[0, :, outer, body, :], 0),
        load(h_in.at[:, outer], hb.at[:, outer, body_h, :], 1),
        load(e_in.at[:, inner], eb.at[0, :, inner, body, :], 2),
        load(h_in.at[:, inner], hb.at[:, inner, body_h, :], 3),
        load(j_in, jb, 4),
        load(p_in, pb, 5),
        load(w_in, wb, 6),
        load(g_in, gi, 7),
        load(r_in, rb, 8),
        load(lvl_in, lvl, 9),
    ]
    for copy in loads:
        copy.start()

    barrier = pltpu.get_barrier_semaphore()

    def greet(device):
        pl.semaphore_signal(barrier, inc=1, device_id=device, device_id_type=MESH)

    pl.when(has_l)(lambda: greet((left, gy)))
    pl.when(has_r)(lambda: greet((right, gy)))
    pl.when(has_l & has_u)(lambda: greet((left, up)))
    pl.when(has_r & has_d)(lambda: greet((right, down)))
    for peer in gather_peers():
        greet(peer)
    for _, peer in scatter_peers():
        greet(peer)

    gho[...] = jnp.zeros(gho.shape, F32)
    zero_row = jnp.zeros((8, LANES), F32)
    for c in range(3):
        for x in range(LX):
            eb[0, c, x, NZ:, :] = zero_row
            eb[1, c, x, NZ:, :] = zero_row
            hb[c, x, 0:8, :] = zero_row
    for step in range(STEPS):
        rxe[step, 1, 0:8, :] = zero_row

    @pl.when(jnp.logical_not(has_r))
    def _():
        rxe[...] = jnp.zeros(rxe.shape, F32)

    @pl.when(jnp.logical_not(has_l))
    def _():
        rxh[...] = jnp.zeros(rxh.shape, F32)

    @pl.when(jnp.logical_not(has_u))
    def _():
        rye[...] = jnp.zeros(rye.shape, F32)

    @pl.when(jnp.logical_not(has_d))
    def _():
        ryh[...] = jnp.zeros(ryh.shape, F32)

    @pl.when(jnp.logical_not(has_l & has_u))
    def _():
        rce[...] = jnp.zeros(rce.shape, F32)

    @pl.when(jnp.logical_not(has_r & has_d))
    def _():
        rch[...] = jnp.zeros(rch.shape, F32)

    edge_l = has_l.astype(F32) * DT
    edge_d = has_d.astype(F32) * DT
    edge_r = has_r.astype(F32) * DT
    edge_u = has_u.astype(F32) * DT
    lane = lax.broadcasted_iota(jnp.int32, (CH, LANES), 1)
    first_lane = lane == 0
    last_lane = lane == LANES - 1

    def remote(src, dst, send, recv, device):
        return pltpu.make_async_remote_copy(
            src_ref=src, dst_ref=dst, send_sem=send, recv_sem=recv,
            device_id=device, device_id_type=MESH,
        )

    def xe_copy(s, par, cut):
        z, zr = pl.ds(cut * CH, CH), pl.ds(8 + cut * CH, CH)
        return remote(
            eb.at[par, pl.ds(1, 2), 0, z, :], rxe.at[s, :, zr, :],
            xe_s.at[s], xe_r.at[s * NCH + cut], (left, gy),
        )

    def xh_copy(s, cut):
        z = pl.ds(cut * CH, CH)
        return remote(
            hs.at[s, :, z, :], rxh.at[s, :, z, :],
            xh_s.at[s], xh_r.at[s * NCH + cut], (right, gy),
        )

    def l1_copy(s):
        return remote(sl.at[s], rye.at[s], l1_s.at[s], ye_r.at[s], (gx, down))

    def l2_copy(s):
        return remote(tl.at[s], rce.at[s], l2_s.at[s], ce_r.at[s], (right, down))

    def r1_copy(s):
        return remote(sr.at[s], ryh.at[s], r1_s.at[s], yh_r.at[s], (gx, up))

    def r2_copy(s):
        return remote(tr.at[s], rch.at[s], r2_s.at[s], ch_r.at[s], (left, up))

    def local_h(par, x, cut):
        z = pl.ds(cut * CH, CH)
        z1 = pl.ds(cut * CH + 1, CH)
        zh = pl.ds(8 + cut * CH, CH)
        ex, ey, ez = eb[par, 0, x, z, :], eb[par, 1, x, z, :], eb[par, 2, x, z, :]
        exz, eyz = eb[par, 0, x, z1, :], eb[par, 1, x, z1, :]
        exy = jnp.where(last_lane, 0.0, pltpu.roll(ex, LANES - 1, 1))
        ezy = jnp.where(last_lane, 0.0, pltpu.roll(ez, LANES - 1, 1))
        hx = hb[0, x, zh, :] - DT * ((ezy - ez) - (eyz - ey))
        if x < LX - 1:
            hy = hb[1, x, zh, :] - DT * ((exz - ex) - (eb[par, 2, x + 1, z, :] - ez))
            hz = hb[2, x, zh, :] - DT * ((eb[par, 1, x + 1, z, :] - ey) - (exy - ex))
        else:
            hy = hb[1, x, zh, :] - DT * ((exz - ex) + ez)
            hz = hb[2, x, zh, :] + DT * (ey + (exy - ex))
        hb[0, x, zh, :] = hx
        hb[1, x, zh, :] = hy
        hb[2, x, zh, :] = hz
        if x == LX - 1:
            return hy, hz
        return hx, hz

    def outer_h(s, par, cut):
        z = pl.ds(cut * CH, CH)
        hs[s, 0, z, :], hs[s, 1, z, :] = local_h(par, LX - 1, cut)

    def turn(value, at, to):
        shift = (to - at) % LANES
        return pltpu.roll(value, shift, 1) if shift else value

    def put(acc, value, at, to):
        return jnp.where(lane == to, turn(value, at, to), acc)

    def drop_rate(x, z, drop):
        wb[x, z, :] = (1.0 - DT * REC) * wb[x, z, :] + pump[x, z, :] - (0.5 * SAT) * drop

    def e_pass(par, x, keep):
        for cut in range(NCH):
            z = pl.ds(cut * CH, CH)
            zh = pl.ds(8 + cut * CH, CH)
            zb = pl.ds(7 + cut * CH, CH)
            ex, ey, ez = eb[par, 0, x, z, :], eb[par, 1, x, z, :], eb[par, 2, x, z, :]
            hx, hy, hz = hb[0, x, zh, :], hb[1, x, zh, :], hb[2, x, zh, :]
            dy_hz = hz - jnp.where(first_lane, edge_d * ex, pltpu.roll(hz, 1, 1))
            dy_hx = hx + jnp.where(first_lane, edge_d * ez, -pltpu.roll(hx, 1, 1))
            if x == 0:
                dx_hz = hz + edge_l * ey
                dx_hy = hy - edge_l * ez
            else:
                dx_hz = hz - hb[2, x - 1, zh, :]
                dx_hy = hy - hb[1, x - 1, zh, :]
            curl_x = dy_hz - (hy - hb[1, x, zb, :])
            curl_y = (hx - hb[0, x, zb, :]) - dx_hz
            curl_z = dx_hy - dy_hx
            inv = wb[x, z, :]
            gain = gb[x, z, :]
            for c, old, curl in ((0, ex, curl_x), (1, ey, curl_y), (2, ez, curl_z)):
                pol = pb[c, x, z, :]
                cur = gain * (keep * jb[c, x, z, :] + (inv * old - pol))
                jb[c, x, z, :] = cur
                pb[c, x, z, :] = pol + cur
                eb[1 - par, c, x, z, :] = old + (DT * curl - cur)

    small_lane = lane % 16
    top_row = lax.broadcasted_iota(jnp.int32, (CH, LANES), 0) == 0
    edge_lanes = first_lane | last_lane

    def fix_y(s, par):
        ye, yh = rye[s], ryh[s]
        ye8, yh8 = pltpu.roll(ye, LANES - 8, 1), pltpu.roll(yh, LANES - 8, 1)
        under = pltpu.roll(ye8, 1, 0)
        under = jnp.where(top_row, jnp.where(lane < 16, 0.0, pltpu.roll(under, 16, 1)), under)
        before = jnp.where(small_lane >= 2, pltpu.roll(ye, 2, 1), 0.0)
        add_x = (DT * DT) * ye - DT * yh8
        add_y = (DT * DT) * ((before - ye) - (ye8 - under))
        add_z = (DT * DT) * ye8 + DT * yh
        new = 1 - par
        for x in (0, 3, 1, 2):
            for cut in range(NCH):
                z = pl.ds(cut * CH, CH)
                zh = pl.ds(8 + cut * CH, CH)
                at = cut * 16 + 2 * x
                eb[new, 0, x, z, :] = eb[new, 0, x, z, :] + jnp.where(edge_lanes, turn(add_x, at, LANES - 1), 0.0)
                eb[new, 1, x, z, :] = eb[new, 1, x, z, :] + jnp.where(last_lane, turn(add_y, at, LANES - 1), 0.0)
                eb[new, 2, x, z, :] = eb[new, 2, x, z, :] + jnp.where(edge_lanes, turn(add_z, at, LANES - 1), 0.0)
                hb[0, x, zh, :] = hb[0, x, zh, :] - jnp.where(last_lane, DT * turn(ye8, at, LANES - 1), 0.0)
                hb[2, x, zh, :] = hb[2, x, zh, :] + jnp.where(last_lane, DT * turn(ye, at, LANES - 1), 0.0)

    def late_inversion(par, x):
        for cut in range(NCH):
            z = pl.ds(cut * CH, CH)
            drop = None
            for c in range(3):
                term = (eb[par, c, x, z, :] + eb[1 - par, c, x, z, :]) * jb[c, x, z, :]
                drop = term if drop is None else drop + term
            drop_rate(x, z, drop)

    def fix_first(s, par, cut):
        z = pl.ds(cut * CH, CH)
        corner = jnp.where(last_lane, (DT * DT) * turn(rce[s], cut * 16, LANES - 1), 0.0)
        eb[1 - par, 1, 0, z, :] = eb[1 - par, 1, 0, z, :] + (DT * rxh[s, 1, z, :] + corner)
        eb[1 - par, 2, 0, z, :] = eb[1 - par, 2, 0, z, :] - DT * rxh[s, 0, z, :]

    def fix_outer(s, par, cut):
        x = LX - 1
        z = pl.ds(cut * CH, CH)
        zh = pl.ds(8 + cut * CH, CH)
        zb = pl.ds(7 + cut * CH, CH)
        ry = DT * rxe[s, 1, zh, :]
        rz = DT * rxe[s, 0, zh, :]
        hb[1, x, zh, :] = hb[1, x, zh, :] + ry
        hb[2, x, zh, :] = hb[2, x, zh, :] - rz
        side = jnp.where(first_lane, DT * turn(rch[s], cut * 16, 0), pltpu.roll(rz, 1, 1))
        back = DT * rxe[s, 1, zb, :]
        eb[1 - par, 0, x, z, :] = eb[1 - par, 0, x, z, :] + DT * ((side - rz) - (ry - back))
        eb[1 - par, 1, x, z, :] = eb[1 - par, 1, x, z, :] + DT * rz
        eb[1 - par, 2, x, z, :] = eb[1 - par, 2, x, z, :] + DT * ry

    def wave_turns(col):
        f = gy * FL + col // LANES
        return (0.6 + 0.05 * f.astype(F32)) * (1.0 / (2.0 * math.pi))

    def direction(index):
        return 0.75 * (2.0 * index.astype(F32) - 63.0) / 63.0

    def build_tables():
        rows = 64

        def y_rows(i, carry):
            row = lax.broadcasted_iota(jnp.int32, (rows, LANES), 0) + i * rows
            col = lax.broadcasted_iota(jnp.int32, (rows, LANES), 1)
            base = (row.astype(F32) - 256.0) * direction(col % 64)
            quarter = jnp.where(col < 64, 0.25, 0.0)
            for f in range(FL):
                wave = (0.6 + 0.05 * (gy * FL + f).astype(F32)) * (1.0 / (2.0 * math.pi))
                high, low = split(sin_turns(wave * base + quarter))
                tab_h[pl.ds(i * rows, rows), f * LANES : (f + 1) * LANES] = high
                tab_l[pl.ds(i * rows, rows), f * LANES : (f + 1) * LANES] = low
            return carry

        lax.fori_loop(0, 512 // rows, y_rows, 0)
        row = lax.broadcasted_iota(jnp.int32, (128, LANES), 0)
        col = lax.broadcasted_iota(jnp.int32, (128, LANES), 1)
        a = 2 * (y_lo * 16 + row // 8) + (row // 4) % 2
        item = col % 64
        group = jnp.where(item < 24, 0, 1)
        r = item - group * 24
        kind = jnp.where(r < 16, r // 4, jnp.where(r == 17, 0, jnp.where(r == 18, 3, 2)))
        place = jnp.where(r < 16, r % 4, jnp.where(r == 16, 4, -1))
        cell = (group * 16 + dest) * 4 + place - 64
        base = cell.astype(F32) * direction(a)
        quarter = jnp.where(col < 64, 0.25, 0.0)
        used = ((row % 4) == kind) & (item < 48) & (r < 20)
        for f in range(FL):
            wave = (0.6 + 0.05 * (gy * FL + f).astype(F32)) * (1.0 / (2.0 * math.pi))
            value = jnp.where(used, sin_turns(wave * base + quarter), 0.0) * (1.0 / 256.0)
            high, low = split(value)
            xt_h[f] = high
            xt_l[f] = low
        inn[...] = jnp.zeros(inn.shape, F32)

    gather_bytes = pl.ds(0, 7)

    def gather_copies(n):
        mine = gat.at[n, gy * 2 + y_lo]
        return [remote(mine, mine, g_s.at[n], g_r.at[n], peer) for peer in gather_peers()]

    def gather_wait(n, sem):
        pltpu.make_async_copy(gat.at[n, gather_bytes], gat.at[n, gather_bytes], sem.at[n]).wait()

    def add_batch(n):
        gather_wait(n, g_r)
        lane8 = lax.broadcasted_iota(jnp.int32, (8, LANES), 1)
        first8, last8 = lane8 == 0, lane8 == LANES - 1
        blocks = []
        for q in range(4):
            tiles = []
            for group in range(2):
                above = gat[n, (q + 1) * 2 + group, 24:32, :] if q < 3 else None
                below = gat[n, (q - 1) * 2 + group, 24:32, :] if q > 0 else None
                for t in range(3):
                    tile = gat[n, q * 2 + group, 8 * t : 8 * t + 8, :]
                    if above is not None:
                        tile = tile + jnp.where(last8, turn(above, 2 * t, 0), 0.0)
                    if below is not None:
                        tile = tile + jnp.where(first8, turn(below, 2 * t, 0), 0.0)
                    tiles.append(tile)
            blocks.append(jnp.concatenate(tiles, axis=0))
        lhs = jnp.concatenate(blocks, axis=1)
        res = dot3(split(lhs), (tab_h[...], tab_l[...]))
        row = lax.broadcasted_iota(jnp.int32, (24, LANES), 0)
        col = lax.broadcasted_iota(jnp.int32, (24, LANES), 1)
        late = jnp.where((row < 8) | (row == 17), 0.5, 1.0) + n.astype(F32)
        sign = jnp.where(col < 64, DT, -DT)
        for f in range(FL):
            wave = (0.6 + 0.05 * (gy * FL + f).astype(F32)) * (1.0 / (2.0 * math.pi))
            turns = wave * DT * late
            real = DT * sin_turns(turns + 0.25)
            imag = sign * sin_turns(turns)
            for group in range(2):
                part = res[group * 24 : (group + 1) * 24, f * LANES : (f + 1) * LANES]
                rows = pl.ds(group * 24, 24)
                inn[rows, f * LANES : (f + 1) * LANES] += real * part + imag * pltpu.roll(part, 64, 1)

    loads[0].wait()
    loads[1].wait()
    for cut in range(NCH - 1, -1, -1):
        outer_h(0, 0, cut)
    loads[2].wait()
    greeted = (
        22
        + has_l.astype(jnp.int32)
        + has_r.astype(jnp.int32)
        + (has_l & has_u).astype(jnp.int32)
        + (has_r & has_d).astype(jnp.int32)
    )
    pl.semaphore_wait(barrier, greeted)

    @pl.when(has_l)
    def _():
        for cut in range(NCH - 1, -1, -1):
            xe_copy(0, 0, cut).start()

    @pl.when(has_r)
    def _():
        for cut in range(NCH - 1, -1, -1):
            xh_copy(0, cut).start()

    def send_corners(s, par):
        left_col = jnp.zeros((CH, LANES), F32)
        right_col = jnp.zeros((CH, LANES), F32)
        for cut in range(NCH):
            z = pl.ds(cut * CH, CH)
            left_col = put(left_col, eb[par, 0, LX - 1, z, :], 0, cut * 16)
            right_col = put(right_col, eb[par, 1, 0, z, :], LANES - 1, cut * 16)
        tl[s] = left_col
        tr[s] = right_col
        pl.when(has_r & has_d)(lambda: l2_copy(s).start())
        pl.when(has_l & has_u)(lambda: r2_copy(s).start())

    def put_low(pack, par, x):
        for cut in range(NCH):
            z = pl.ds(cut * CH, CH)
            pack = put(pack, eb[par, 0, x, z, :], 0, cut * 16 + 2 * x)
            pack = put(pack, eb[par, 2, x, z, :], 0, cut * 16 + 8 + 2 * x)
        return pack

    def put_high(pack, par, x):
        for cut in range(NCH):
            if x < LX - 1:
                hx, hz = local_h(par, x, cut)
            else:
                zh = pl.ds(8 + cut * CH, CH)
                hx, hz = hb[0, x, zh, :], hb[2, x, zh, :]
            pack = put(pack, hx, LANES - 1, cut * 16 + 2 * x + 1)
            pack = put(pack, hz, LANES - 1, cut * 16 + 8 + 2 * x + 1)
        return pack

    def early_pack(s, par):
        none = jnp.zeros((CH, LANES), F32)
        sl[s] = put_low(put_low(none, par, 1), par, 2)
        sr[s] = put_high(none, par, 1)

    def late_pack(s, par):
        sl[s] = put_low(put_low(sl[s], par, 0), par, 3)
        pl.when(has_d)(lambda: l1_copy(s).start())
        sr[s] = put_high(put_high(put_high(sr[s], par, 3), par, 0), par, 2)
        pl.when(has_u)(lambda: r1_copy(s).start())

    send_corners(0, 0)
    loads[3].wait()
    early_pack(0, 0)

    def far_slab(s, par, keep):
        me = gy * 2 + y_lo
        z, zl, zh, zb = pl.ds(NZ - 8, 8), pl.ds(NZ - 9, 8), pl.ds(NZ, 8), pl.ds(NZ - 1, 8)
        lane8 = lax.broadcasted_iota(jnp.int32, (8, LANES), 1)
        first8, last8 = lane8 == 0, lane8 == LANES - 1
        nothing = jnp.zeros((8, LANES), F32)

        def show(row, value):
            gat[s, me, row : row + 1, :] = value[7:8, :]

        def ghost(row, low, high):
            value = nothing
            if low is not None:
                value = jnp.where(last8, pltpu.roll(low, LANES - 1, 1), value)
            if high is not None:
                value = jnp.where(first8, pltpu.roll(high, 1, 1), value)
            gho[row : row + 1, :] = value[7:8, :]

        gat[s, me, 16:24, :] = nothing
        for x in range(LX):
            ex, ey, ez = eb[par, 0, x, z, :], eb[par, 1, x, z, :], eb[par, 2, x, z, :]
            hx, hy, hz = hb[0, x, zh, :], hb[1, x, zh, :], hb[2, x, zh, :]
            dy_hz = hz - jnp.where(first8, edge_d * ex, pltpu.roll(hz, 1, 1))
            dx_hz = hz + edge_l * ey if x == 0 else hz - hb[2, x - 1, zh, :]
            curl_x = dy_hz - (hy - hb[1, x, zb, :])
            curl_y = (hx - hb[0, x, zb, :]) - dx_hz
            inv, gain = wb[x, z, :], gb[x, z, :]
            cur_x = gain * (keep * jb[0, x, z, :] + (inv * ex - pb[0, x, z, :]))
            cur_y = gain * (keep * jb[1, x, z, :] + (inv * ey - pb[1, x, z, :]))
            show(x, -hy)
            show(4 + x, hx)
            show(8 + x, ey + (DT * curl_y - cur_y))
            show(12 + x, -(ex + (DT * curl_x - cur_x)))
            rise = ez - eb[par, 2, x, zl, :]
            side = -rise - ex if x == 0 else eb[par, 0, x - 1, z, :] - rise - ex
            ghost(4 + x, -edge_d * ez, None)
            ghost(8 + x, (DT * edge_d) * side, None)
            ghost(12 + x, -(DT * edge_d) * ex, edge_u * hz)
            if x == LX - 1:
                show(16, edge_r * hz)
                ghost(16, (edge_r * edge_d) * ex, None)
            if x == 0:
                rz = edge_l * ey
                before = jnp.where(first8, 0.0, pltpu.roll(rz, 1, 1))
                show(17, -edge_l * ez)
                show(18, DT * ((rz - before) + edge_l * rise))
                show(19, DT * rz)
                ghost(18, None, -edge_u * rz)
        gat[s, me, 24:32, :] = (
            gho[0:8, :] + pltpu.roll(gho[8:16, :], 2, 1) + pltpu.roll(gho[16:24, :], 4, 1)
        )

    def gather_start(s):
        for copy in gather_copies(s):
            copy.start()

    def step(s, carry):
        s = jnp.asarray(s, jnp.int32)
        par = s % 2
        more = s < STEPS - 1
        late_pack(s, par)

        @pl.when(s == 0)
        def _():
            for copy in loads[4:]:
                copy.wait()
            for x in range(LX):
                for cut in range(NCH):
                    z = pl.ds(cut * CH, CH)
                    region = rb[x, z, :]
                    rate = jnp.zeros((CH, LANES), F32)
                    for k in range(8):
                        rate = jnp.where(region == k, lvl[k], rate)
                    pump[x, z, :] = (DT * REC) * rate
                    gb[x, z, :] = SCALE * gi[x, z, :].astype(F32)

        @pl.when(s > 0)
        def _():
            for x in range(LX):
                late_inversion(par, x)

        keep = jnp.where(s == 0, KEEP * DT, KEEP)
        far_slab(s, par, keep)
        gather_start(s)
        for x in (0, 3, 1, 2):
            e_pass(par, x, keep)
        pl.when(s == 0)(build_tables)
        pl.when(s > 0)(lambda: add_batch(s - 1))

        pl.when(has_u)(lambda: l1_copy(s).wait_recv())
        pl.when(has_d)(lambda: r1_copy(s).wait_recv())
        fix_y(s, par)

        pl.when(more)(lambda: early_pack(s + 1, 1 - par))

        pl.when(has_r & has_d)(lambda: r2_copy(s).wait_recv())
        pl.when(has_l & has_u)(lambda: l2_copy(s).wait_recv())

        def next_low(cut):
            pl.when(more & has_l)(lambda: xe_copy(s + 1, 1 - par, cut).start())

        def next_high(cut):
            @pl.when(more)
            def _():
                outer_h(s + 1, 1 - par, cut)
                pl.when(has_r)(lambda: xh_copy(s + 1, cut).start())

        for cut in range(NCH - 1, -1, -1):
            pl.when(has_l)(lambda: xh_copy(s, cut).wait_recv())
            fix_first(s, par, cut)
            if cut > 0:
                next_low(cut)
            pl.when(has_r)(lambda: xe_copy(s, par, cut).wait_recv())
            if cut < NCH - 1:
                fix_outer(s, par, cut + 1)
            if 0 < cut < NCH - 1:
                next_high(cut + 1)
        fix_outer(s, par, 0)
        pl.when(more)(lambda: send_corners(s + 1, 1 - par))
        next_low(0)
        next_high(1)
        next_high(0)

        @pl.when(has_l)
        def _():
            whole = eb.at[par, pl.ds(1, 2), 0, body, :]
            remote(whole, rxe.at[s, :, body_h, :], xe_s.at[s], xe_r.at[0], (left, gy)).wait_send()

        @pl.when(has_r)
        def _():
            remote(hs.at[s], rxh.at[s], xh_s.at[s], xh_r.at[0], (right, gy)).wait_send()

        pl.when(has_d)(lambda: l1_copy(s).wait_send())
        pl.when(has_u)(lambda: r1_copy(s).wait_send())
        pl.when(has_r & has_d)(lambda: l2_copy(s).wait_send())
        pl.when(has_l & has_u)(lambda: r2_copy(s).wait_send())
        return carry

    lax.fori_loop(0, STEPS, step, 0)

    final = pltpu.make_async_copy(eb.at[0, :, :, body, :], out_e, out_sem)
    final.start()
    add_batch(jnp.int32(STEPS - 1))

    col = lax.broadcasted_iota(jnp.int32, (48, LANES), 1)
    sign = jnp.where(col < 64, -1.0, 1.0)
    filler = jnp.zeros((16, LANES), F32)
    for f in range(FL):
        part = inn[:, f * LANES : (f + 1) * LANES]
        rhs = jnp.concatenate([part, filler, sign * pltpu.roll(part, 64, 1), filler], axis=0)
        res = dot3((xt_h[f], xt_l[f]), split(rhs))
        for d in range(16):
            sbuf[d, f] = res[8 * d : 8 * d + 8, :]

    scatter = [
        remote(sbuf.at[to], rbuf.at[dest], rs_s, rs_r, peer) for to, peer in scatter_peers()
    ]
    for copy in scatter:
        copy.start()
    rbuf[dest] = sbuf[dest]
    fifteen = pl.ds(0, 15)
    pltpu.make_async_copy(rbuf.at[fifteen], rbuf.at[fifteen], rs_r).wait()

    low_half = lax.broadcasted_iota(jnp.int32, (1, LANES), 1) < 64
    for f in range(FL):
        total = rbuf[0, f]
        for d in range(1, 16):
            total = total + rbuf[d, f]
        turned = pltpu.roll(total, 64, 1)
        for a in range(2):
            for pair in range(2):
                r0, r1 = a * 4 + 2 * pair, a * 4 + 2 * pair + 1
                real = jnp.where(low_half, total[r0 : r0 + 1, :], turned[r1 : r1 + 1, :])
                imag = jnp.where(low_half, turned[r0 : r0 + 1, :], total[r1 : r1 + 1, :])
                out_f[a, f : f + 1, pair * LANES : (pair + 1) * LANES] = real
                out_f[a, f : f + 1, 256 + pair * LANES : 256 + (pair + 1) * LANES] = imag

    pltpu.make_async_copy(sbuf.at[fifteen], sbuf.at[fifteen], rs_s).wait()

    def settle(n, carry):
        gather_wait(n, g_s)
        return carry

    lax.fori_loop(0, STEPS, settle, 0)
    final.wait()


def local(electric, magnetic, polarization, current, inversion, gain_mask, pump_region, pump_level):
    far_memory = pl.BlockSpec(memory_space=pltpu.HBM)
    near_memory = pl.BlockSpec(memory_space=pltpu.VMEM)
    dma = pltpu.SemaphoreType.DMA
    vmem = pltpu.VMEM
    state = (3, LX, NZ, LANES)
    operands = [
        pltpu.with_memory_space_constraint(operand, pltpu.HBM)
        for operand in (
            electric, magnetic, polarization, current, inversion, gain_mask, pump_region, pump_level,
        )
    ]
    return pl.pallas_call(
        kernel,
        out_shape=(
            jax.ShapeDtypeStruct(state, F32),
            jax.ShapeDtypeStruct((2, FL, 512), F32),
        ),
        in_specs=[far_memory] * 8,
        out_specs=(near_memory, near_memory),
        scratch_shapes=[
            vmem((2, 3, LX, NZ + 8, LANES), F32),
            vmem((3, LX, NZ + 8, LANES), F32),
            vmem(state, F32),
            vmem(state, F32),
            vmem(state[1:], F32),
            vmem(state[1:], jnp.int32),
            vmem(state[1:], F32),
            vmem(state[1:], jnp.int32),
            vmem(state[1:], F32),
            vmem((STEPS, 2, NZ, LANES), F32),
            vmem((STEPS, 2, NZ + 8, LANES), F32),
            vmem((STEPS, 2, NZ, LANES), F32),
            vmem((STEPS, CH, LANES), F32),
            vmem((STEPS, CH, LANES), F32),
            vmem((STEPS, CH, LANES), F32),
            vmem((STEPS, CH, LANES), F32),
            vmem((STEPS, CH, LANES), F32),
            vmem((STEPS, CH, LANES), F32),
            vmem((STEPS, CH, LANES), F32),
            vmem((STEPS, CH, LANES), F32),
            vmem((STEPS, 8, 32, LANES), F32),
            vmem((24, LANES), F32),
            vmem((512, FL * LANES), BF16),
            vmem((512, FL * LANES), BF16),
            vmem((FL, 128, LANES), BF16),
            vmem((FL, 128, LANES), BF16),
            vmem((48, FL * LANES), F32),
            vmem((16, FL, 8, LANES), F32),
            vmem((16, FL, 8, LANES), F32),
            pltpu.SMEM((8,), F32),
            dma((10,)),
            dma((STEPS,)),
            dma((STEPS * NCH,)),
            dma((STEPS,)),
            dma((STEPS * NCH,)),
        ]
        + [dma((STEPS,))] * 10
        + [dma, dma, dma],
        compiler_params=pltpu.CompilerParams(
            collective_id=0, has_side_effects=True, vmem_limit_bytes=24 << 20
        ),
    )(*operands)


def solution(mesh):
    return jax.shard_map(
        local,
        mesh=mesh,
        in_specs=(
            P(None, "gx", None, "gy"),
            P(None, "gx", None, "gy"),
            P(None, "gx", None, "gy"),
            P(None, "gx", None, "gy"),
            P("gx", None, "gy"),
            P("gx", None, "gy"),
            P("gx", None, "gy"),
            P(),
        ),
        out_specs=(P(None, "gx", None, "gy"), P("gx", "gy", None)),
        check_vma=False,
    )
```

```python
import functools
import math

import jax
import jax.numpy as jnp
from jax import lax
from jax.experimental import pallas as pl
from jax.experimental.pallas import tpu as pltpu
from jax.sharding import PartitionSpec as P

MESH = pl.DeviceIdType.MESH
F32 = jnp.float32
BF16 = jnp.bfloat16

STEPS = 4
NZ = 96
LX = 4
LANES = 128
CH = 32
NCH = NZ // CH
FL = 4

DT = 0.5
DAMP = 0.4
SAT = 0.5
REC = 0.8
SCALE = DT * DT / (1.0 + 0.5 * DAMP * DT)
KEEP = (1.0 - 0.5 * DAMP * DT) / (DT * DT)


def sin_turns(turns):
    r = turns - jnp.floor(turns + 0.5)
    x = r * (2.0 * math.pi)
    s = x * x
    acc = jnp.full_like(s, 1.0 / math.factorial(17))
    for order, sign in ((15, -1.0), (13, 1.0), (11, -1.0), (9, 1.0), (7, -1.0), (5, 1.0), (3, -1.0), (1, 1.0)):
        acc = acc * s + sign / math.factorial(order)
    return acc * x


def split(value):
    high = value.astype(BF16)
    return high, (value - high.astype(F32)).astype(BF16)


def dot3(a, b):
    ah, al = a
    bh, bl = b
    dot = functools.partial(jnp.dot, preferred_element_type=F32)
    return dot(ah, bh) + dot(al, bh) + dot(ah, bl)


def kernel(
    e_in, h_in, p_in, j_in, w_in, g_in, r_in, lvl_in,
    out_e, out_f,
    eb, hb, jb, pb, wb, gi, gb, rb, pump,
    hs, rxe, rxh, rye, ryh, rce, rch, sl, sr, tl, tr,
    gat, gho, tab_h, tab_l, xt_h, xt_l, inn, sbuf, rbuf,
    lvl, load_sem, xe_s, xe_r, xh_s, xh_r, l1_s, l2_s, r1_s, r2_s,
    ye_r, yh_r, ce_r, ch_r, g_s, g_r, rs_s, rs_r, out_sem,
):
    gx = lax.axis_index("gx")
    gy = lax.axis_index("gy")
    y_lo = gx // 16
    xc = (gx // 4) % 4
    zc = gx % 4
    left, right = (gx + 31) % 32, (gx + 1) % 32
    down, up = (gy + 3) % 4, (gy + 1) % 4
    has_l, has_r = gx > 0, gx < 31
    has_d, has_u = gy > 0, gy < 3
    dest = xc * 4 + zc

    def gather_peers():
        for dl in range(2):
            for dy in range(4):
                if dl or dy:
                    yield ((gx + 16 * dl) % 32, (gy + dy) % 4)

    def scatter_peers():
        for d in range(1, 16):
            to = (dest + d) % 16
            yield to, (y_lo * 16 + to, gy)

    def load(src, dst, index):
        return pltpu.make_async_copy(src, dst, load_sem.at[index])

    body, body_h = pl.ds(0, NZ), pl.ds(8, NZ)
    inner, outer = pl.ds(0, LX - 1), pl.ds(LX - 1, 1)
    loads = [
        load(e_in.at[:, outer], eb.at[0, :, outer, body, :], 0),
        load(h_in.at[:, outer], hb.at[:, outer, body_h, :], 1),
        load(e_in.at[:, inner], eb.at[0, :, inner, body, :], 2),
        load(h_in.at[:, inner], hb.at[:, inner, body_h, :], 3),
        load(j_in, jb, 4),
        load(p_in, pb, 5),
        load(w_in, wb, 6),
        load(g_in, gi, 7),
        load(r_in, rb, 8),
        load(lvl_in, lvl, 9),
    ]
    for copy in loads:
        copy.start()

    barrier = pltpu.get_barrier_semaphore()

    def greet(device):
        pl.semaphore_signal(barrier, inc=1, device_id=device, device_id_type=MESH)

    pl.when(has_l)(lambda: greet((left, gy)))
    pl.when(has_r)(lambda: greet((right, gy)))
    pl.when(has_l & has_u)(lambda: greet((left, up)))
    pl.when(has_r & has_d)(lambda: greet((right, down)))
    for peer in gather_peers():
        greet(peer)
    for _, peer in scatter_peers():
        greet(peer)

    gho[...] = jnp.zeros(gho.shape, F32)
    zero_row = jnp.zeros((8, LANES), F32)
    for c in range(3):
        for x in range(LX):
            eb[0, c, x, NZ:, :] = zero_row
            eb[1, c, x, NZ:, :] = zero_row
            hb[c, x, 0:8, :] = zero_row
    for step in range(STEPS):
        rxe[step, 1, 0:8, :] = zero_row

    @pl.when(jnp.logical_not(has_r))
    def _():
        rxe[...] = jnp.zeros(rxe.shape, F32)

    @pl.when(jnp.logical_not(has_l))
    def _():
        rxh[...] = jnp.zeros(rxh.shape, F32)

    @pl.when(jnp.logical_not(has_u))
    def _():
        rye[...] = jnp.zeros(rye.shape, F32)

    @pl.when(jnp.logical_not(has_d))
    def _():
        ryh[...] = jnp.zeros(ryh.shape, F32)

    @pl.when(jnp.logical_not(has_l & has_u))
    def _():
        rce[...] = jnp.zeros(rce.shape, F32)

    @pl.when(jnp.logical_not(has_r & has_d))
    def _():
        rch[...] = jnp.zeros(rch.shape, F32)

    edge_l = has_l.astype(F32) * DT
    edge_d = has_d.astype(F32) * DT
    edge_r = has_r.astype(F32) * DT
    edge_u = has_u.astype(F32) * DT
    lane = lax.broadcasted_iota(jnp.int32, (CH, LANES), 1)
    first_lane = lane == 0
    last_lane = lane == LANES - 1

    def remote(src, dst, send, recv, device):
        return pltpu.make_async_remote_copy(
            src_ref=src, dst_ref=dst, send_sem=send, recv_sem=recv,
            device_id=device, device_id_type=MESH,
        )

    def xe_copy(s, par, cut):
        z, zr = pl.ds(cut * CH, CH), pl.ds(8 + cut * CH, CH)
        return remote(
            eb.at[par, pl.ds(1, 2), 0, z, :], rxe.at[s, :, zr, :],
            xe_s.at[s], xe_r.at[s * NCH + cut], (left, gy),
        )

    def xh_copy(s, cut):
        z = pl.ds(cut * CH, CH)
        return remote(
            hs.at[s, :, z, :], rxh.at[s, :, z, :],
            xh_s.at[s], xh_r.at[s * NCH + cut], (right, gy),
        )

    def l1_copy(s):
        return remote(sl.at[s], rye.at[s], l1_s.at[s], ye_r.at[s], (gx, down))

    def l2_copy(s):
        return remote(tl.at[s], rce.at[s], l2_s.at[s], ce_r.at[s], (right, down))

    def r1_copy(s):
        return remote(sr.at[s], ryh.at[s], r1_s.at[s], yh_r.at[s], (gx, up))

    def r2_copy(s):
        return remote(tr.at[s], rch.at[s], r2_s.at[s], ch_r.at[s], (left, up))

    def local_h(par, x, cut):
        z = pl.ds(cut * CH, CH)
        z1 = pl.ds(cut * CH + 1, CH)
        zh = pl.ds(8 + cut * CH, CH)
        ex, ey, ez = eb[par, 0, x, z, :], eb[par, 1, x, z, :], eb[par, 2, x, z, :]
        exz, eyz = eb[par, 0, x, z1, :], eb[par, 1, x, z1, :]
        exy = jnp.where(last_lane, 0.0, pltpu.roll(ex, LANES - 1, 1))
        ezy = jnp.where(last_lane, 0.0, pltpu.roll(ez, LANES - 1, 1))
        hx = hb[0, x, zh, :] - DT * ((ezy - ez) - (eyz - ey))
        if x < LX - 1:
            hy = hb[1, x, zh, :] - DT * ((exz - ex) - (eb[par, 2, x + 1, z, :] - ez))
            hz = hb[2, x, zh, :] - DT * ((eb[par, 1, x + 1, z, :] - ey) - (exy - ex))
        else:
            hy = hb[1, x, zh, :] - DT * ((exz - ex) + ez)
            hz = hb[2, x, zh, :] + DT * (ey + (exy - ex))
        hb[0, x, zh, :] = hx
        hb[1, x, zh, :] = hy
        hb[2, x, zh, :] = hz
        if x == LX - 1:
            return hy, hz
        return hx, hz

    def outer_h(s, par, cut):
        z = pl.ds(cut * CH, CH)
        hs[s, 0, z, :], hs[s, 1, z, :] = local_h(par, LX - 1, cut)

    def turn(value, at, to):
        shift = (to - at) % LANES
        return pltpu.roll(value, shift, 1) if shift else value

    def put(acc, value, at, to):
        return jnp.where(lane == to, turn(value, at, to), acc)

    def drop_rate(x, z, drop):
        wb[x, z, :] = (1.0 - DT * REC) * wb[x, z, :] + pump[x, z, :] - (0.5 * SAT) * drop

    def e_pass(par, x, keep):
        for cut in range(NCH):
            z = pl.ds(cut * CH, CH)
            zh = pl.ds(8 + cut * CH, CH)
            zb = pl.ds(7 + cut * CH, CH)
            ex, ey, ez = eb[par, 0, x, z, :], eb[par, 1, x, z, :], eb[par, 2, x, z, :]
            hx, hy, hz = hb[0, x, zh, :], hb[1, x, zh, :], hb[2, x, zh, :]
            dy_hz = hz - jnp.where(first_lane, edge_d * ex, pltpu.roll(hz, 1, 1))
            dy_hx = hx + jnp.where(first_lane, edge_d * ez, -pltpu.roll(hx, 1, 1))
            if x == 0:
                dx_hz = hz + edge_l * ey
                dx_hy = hy - edge_l * ez
            else:
                dx_hz = hz - hb[2, x - 1, zh, :]
                dx_hy = hy - hb[1, x - 1, zh, :]
            curl_x = dy_hz - (hy - hb[1, x, zb, :])
            curl_y = (hx - hb[0, x, zb, :]) - dx_hz
            curl_z = dx_hy - dy_hx
            inv = wb[x, z, :]
            gain = gb[x, z, :]
            for c, old, curl in ((0, ex, curl_x), (1, ey, curl_y), (2, ez, curl_z)):
                pol = pb[c, x, z, :]
                cur = gain * (keep * jb[c, x, z, :] + (inv * old - pol))
                jb[c, x, z, :] = cur
                pb[c, x, z, :] = pol + cur
                eb[1 - par, c, x, z, :] = old + (DT * curl - cur)

    small_lane = lane % 16
    top_row = lax.broadcasted_iota(jnp.int32, (CH, LANES), 0) == 0
    edge_lanes = first_lane | last_lane

    def fix_y(s, par):
        ye, yh = rye[s], ryh[s]
        ye8, yh8 = pltpu.roll(ye, LANES - 8, 1), pltpu.roll(yh, LANES - 8, 1)
        under = pltpu.roll(ye8, 1, 0)
        under = jnp.where(top_row, jnp.where(lane < 16, 0.0, pltpu.roll(under, 16, 1)), under)
        before = jnp.where(small_lane >= 2, pltpu.roll(ye, 2, 1), 0.0)
        add_x = (DT * DT) * ye - DT * yh8
        add_y = (DT * DT) * ((before - ye) - (ye8 - under))
        add_z = (DT * DT) * ye8 + DT * yh
        new = 1 - par
        for x in (0, 3, 1, 2):
            for cut in range(NCH):
                z = pl.ds(cut * CH, CH)
                zh = pl.ds(8 + cut * CH, CH)
                at = cut * 16 + 2 * x
                eb[new, 0, x, z, :] = eb[new, 0, x, z, :] + jnp.where(edge_lanes, turn(add_x, at, LANES - 1), 0.0)
                eb[new, 1, x, z, :] = eb[new, 1, x, z, :] + jnp.where(last_lane, turn(add_y, at, LANES - 1), 0.0)
                eb[new, 2, x, z, :] = eb[new, 2, x, z, :] + jnp.where(edge_lanes, turn(add_z, at, LANES - 1), 0.0)
                hb[0, x, zh, :] = hb[0, x, zh, :] - jnp.where(last_lane, DT * turn(ye8, at, LANES - 1), 0.0)
                hb[2, x, zh, :] = hb[2, x, zh, :] + jnp.where(last_lane, DT * turn(ye, at, LANES - 1), 0.0)

    def late_inversion(par, x, cuts):
        for cut in cuts:
            z = pl.ds(cut * CH, CH)
            drop = None
            for c in range(3):
                term = (eb[par, c, x, z, :] + eb[1 - par, c, x, z, :]) * jb[c, x, z, :]
                drop = term if drop is None else drop + term
            drop_rate(x, z, drop)

    def fix_first(s, par, cut):
        z = pl.ds(cut * CH, CH)
        corner = jnp.where(last_lane, (DT * DT) * turn(rce[s], cut * 16, LANES - 1), 0.0)
        eb[1 - par, 1, 0, z, :] = eb[1 - par, 1, 0, z, :] + (DT * rxh[s, 1, z, :] + corner)
        eb[1 - par, 2, 0, z, :] = eb[1 - par, 2, 0, z, :] - DT * rxh[s, 0, z, :]

    def fix_outer(s, par, cut):
        x = LX - 1
        z = pl.ds(cut * CH, CH)
        zh = pl.ds(8 + cut * CH, CH)
        zb = pl.ds(7 + cut * CH, CH)
        ry = DT * rxe[s, 1, zh, :]
        rz = DT * rxe[s, 0, zh, :]
        hb[1, x, zh, :] = hb[1, x, zh, :] + ry
        hb[2, x, zh, :] = hb[2, x, zh, :] - rz
        side = jnp.where(first_lane, DT * turn(rch[s], cut * 16, 0), pltpu.roll(rz, 1, 1))
        back = DT * rxe[s, 1, zb, :]
        eb[1 - par, 0, x, z, :] = eb[1 - par, 0, x, z, :] + DT * ((side - rz) - (ry - back))
        eb[1 - par, 1, x, z, :] = eb[1 - par, 1, x, z, :] + DT * rz
        eb[1 - par, 2, x, z, :] = eb[1 - par, 2, x, z, :] + DT * ry

    def wave_turns(col):
        f = gy * FL + col // LANES
        return (0.6 + 0.05 * f.astype(F32)) * (1.0 / (2.0 * math.pi))

    def direction(index):
        return 0.75 * (2.0 * index.astype(F32) - 63.0) / 63.0

    def build_tables():
        rows = 64

        def y_rows(i, carry):
            row = lax.broadcasted_iota(jnp.int32, (rows, LANES), 0) + i * rows
            col = lax.broadcasted_iota(jnp.int32, (rows, LANES), 1)
            base = (row.astype(F32) - 256.0) * direction(col % 64)
            quarter = jnp.where(col < 64, 0.25, 0.0)
            for f in range(FL):
                wave = (0.6 + 0.05 * (gy * FL + f).astype(F32)) * (1.0 / (2.0 * math.pi))
                high, low = split(sin_turns(wave * base + quarter))
                tab_h[pl.ds(i * rows, rows), f * LANES : (f + 1) * LANES] = high
                tab_l[pl.ds(i * rows, rows), f * LANES : (f + 1) * LANES] = low
            return carry

        lax.fori_loop(0, 512 // rows, y_rows, 0)
        row = lax.broadcasted_iota(jnp.int32, (128, LANES), 0)
        col = lax.broadcasted_iota(jnp.int32, (128, LANES), 1)
        a = 2 * (y_lo * 16 + row // 8) + (row // 4) % 2
        item = col % 64
        group = jnp.where(item < 24, 0, 1)
        r = item - group * 24
        kind = jnp.where(r < 16, r // 4, jnp.where(r == 17, 0, jnp.where(r == 18, 3, 2)))
        place = jnp.where(r < 16, r % 4, jnp.where(r == 16, 4, -1))
        cell = (group * 16 + dest) * 4 + place - 64
        base = cell.astype(F32) * direction(a)
        quarter = jnp.where(col < 64, 0.25, 0.0)
        used = ((row % 4) == kind) & (item < 48) & (r < 20)
        for f in range(FL):
            wave = (0.6 + 0.05 * (gy * FL + f).astype(F32)) * (1.0 / (2.0 * math.pi))
            value = jnp.where(used, sin_turns(wave * base + quarter), 0.0) * (1.0 / 256.0)
            high, low = split(value)
            xt_h[f] = high
            xt_l[f] = low
        inn[...] = jnp.zeros(inn.shape, F32)

    gather_bytes = pl.ds(0, 7)

    def gather_copies(n):
        mine = gat.at[n, gy * 2 + y_lo]
        return [remote(mine, mine, g_s.at[n], g_r.at[n], peer) for peer in gather_peers()]

    def gather_wait(n, sem):
        pltpu.make_async_copy(gat.at[n, gather_bytes], gat.at[n, gather_bytes], sem.at[n]).wait()

    def add_batch(n):
        gather_wait(n, g_r)
        lane8 = lax.broadcasted_iota(jnp.int32, (8, LANES), 1)
        first8, last8 = lane8 == 0, lane8 == LANES - 1
        blocks = []
        for q in range(4):
            tiles = []
            for group in range(2):
                above = gat[n, (q + 1) * 2 + group, 24:32, :] if q < 3 else None
                below = gat[n, (q - 1) * 2 + group, 24:32, :] if q > 0 else None
                for t in range(3):
                    tile = gat[n, q * 2 + group, 8 * t : 8 * t + 8, :]
                    if above is not None:
                        tile = tile + jnp.where(last8, turn(above, 2 * t, 0), 0.0)
                    if below is not None:
                        tile = tile + jnp.where(first8, turn(below, 2 * t, 0), 0.0)
                    tiles.append(tile)
            blocks.append(jnp.concatenate(tiles, axis=0))
        lhs = jnp.concatenate(blocks, axis=1)
        res = dot3(split(lhs), (tab_h[...], tab_l[...]))
        row = lax.broadcasted_iota(jnp.int32, (24, LANES), 0)
        col = lax.broadcasted_iota(jnp.int32, (24, LANES), 1)
        late = jnp.where((row < 8) | (row == 17), 0.5, 1.0) + n.astype(F32)
        sign = jnp.where(col < 64, DT, -DT)
        for f in range(FL):
            wave = (0.6 + 0.05 * (gy * FL + f).astype(F32)) * (1.0 / (2.0 * math.pi))
            turns = wave * DT * late
            real = DT * sin_turns(turns + 0.25)
            imag = sign * sin_turns(turns)
            for group in range(2):
                part = res[group * 24 : (group + 1) * 24, f * LANES : (f + 1) * LANES]
                rows = pl.ds(group * 24, 24)
                inn[rows, f * LANES : (f + 1) * LANES] += real * part + imag * pltpu.roll(part, 64, 1)

    loads[0].wait()
    loads[1].wait()
    for cut in range(NCH - 1, -1, -1):
        outer_h(0, 0, cut)
    loads[2].wait()
    greeted = (
        22
        + has_l.astype(jnp.int32)
        + has_r.astype(jnp.int32)
        + (has_l & has_u).astype(jnp.int32)
        + (has_r & has_d).astype(jnp.int32)
    )
    pl.semaphore_wait(barrier, greeted)

    @pl.when(has_l)
    def _():
        for cut in range(NCH - 1, -1, -1):
            xe_copy(0, 0, cut).start()

    @pl.when(has_r)
    def _():
        for cut in range(NCH - 1, -1, -1):
            xh_copy(0, cut).start()

    def send_corners(s, par):
        left_col = jnp.zeros((CH, LANES), F32)
        right_col = jnp.zeros((CH, LANES), F32)
        for cut in range(NCH):
            z = pl.ds(cut * CH, CH)
            left_col = put(left_col, eb[par, 0, LX - 1, z, :], 0, cut * 16)
            right_col = put(right_col, eb[par, 1, 0, z, :], LANES - 1, cut * 16)
        tl[s] = left_col
        tr[s] = right_col
        pl.when(has_r & has_d)(lambda: l2_copy(s).start())
        pl.when(has_l & has_u)(lambda: r2_copy(s).start())

    def put_low(pack, par, x):
        for cut in range(NCH):
            z = pl.ds(cut * CH, CH)
            pack = put(pack, eb[par, 0, x, z, :], 0, cut * 16 + 2 * x)
            pack = put(pack, eb[par, 2, x, z, :], 0, cut * 16 + 8 + 2 * x)
        return pack

    def put_high(pack, par, x, done=False):
        for cut in range(NCH):
            if x < LX - 1 and not done:
                hx, hz = local_h(par, x, cut)
            else:
                zh = pl.ds(8 + cut * CH, CH)
                hx, hz = hb[0, x, zh, :], hb[2, x, zh, :]
            pack = put(pack, hx, LANES - 1, cut * 16 + 2 * x + 1)
            pack = put(pack, hz, LANES - 1, cut * 16 + 8 + 2 * x + 1)
        return pack

    def early_pack(s, par):
        none = jnp.zeros((CH, LANES), F32)
        sl[s] = put_low(put_low(none, par, 1), par, 2)
        sr[s] = put_high(none, par, 1)

    def late_pack(s, par, done=False):
        sl[s] = put_low(put_low(sl[s], par, 0), par, 3)
        pl.when(has_d)(lambda: l1_copy(s).start())
        sr[s] = put_high(put_high(put_high(sr[s], par, 3), par, 0, done), par, 2, done)
        pl.when(has_u)(lambda: r1_copy(s).start())

    send_corners(0, 0)
    loads[3].wait()
    early_pack(0, 0)

    def far_slab(s, par, keep):
        me = gy * 2 + y_lo
        z, zl, zh, zb = pl.ds(NZ - 8, 8), pl.ds(NZ - 9, 8), pl.ds(NZ, 8), pl.ds(NZ - 1, 8)
        lane8 = lax.broadcasted_iota(jnp.int32, (8, LANES), 1)
        first8, last8 = lane8 == 0, lane8 == LANES - 1
        nothing = jnp.zeros((8, LANES), F32)

        def show(row, value):
            gat[s, me, row : row + 1, :] = value[7:8, :]

        def ghost(row, low, high):
            value = nothing
            if low is not None:
                value = jnp.where(last8, pltpu.roll(low, LANES - 1, 1), value)
            if high is not None:
                value = jnp.where(first8, pltpu.roll(high, 1, 1), value)
            gho[row : row + 1, :] = value[7:8, :]

        gat[s, me, 16:24, :] = nothing
        for x in range(LX):
            ex, ey, ez = eb[par, 0, x, z, :], eb[par, 1, x, z, :], eb[par, 2, x, z, :]
            hx, hy, hz = hb[0, x, zh, :], hb[1, x, zh, :], hb[2, x, zh, :]
            dy_hz = hz - jnp.where(first8, edge_d * ex, pltpu.roll(hz, 1, 1))
            dx_hz = hz + edge_l * ey if x == 0 else hz - hb[2, x - 1, zh, :]
            curl_x = dy_hz - (hy - hb[1, x, zb, :])
            curl_y = (hx - hb[0, x, zb, :]) - dx_hz
            inv, gain = wb[x, z, :], gb[x, z, :]
            cur_x = gain * (keep * jb[0, x, z, :] + (inv * ex - pb[0, x, z, :]))
            cur_y = gain * (keep * jb[1, x, z, :] + (inv * ey - pb[1, x, z, :]))
            show(x, -hy)
            show(4 + x, hx)
            show(8 + x, ey + (DT * curl_y - cur_y))
            show(12 + x, -(ex + (DT * curl_x - cur_x)))
            rise = ez - eb[par, 2, x, zl, :]
            side = -rise - ex if x == 0 else eb[par, 0, x - 1, z, :] - rise - ex
            ghost(4 + x, -edge_d * ez, None)
            ghost(8 + x, (DT * edge_d) * side, None)
            ghost(12 + x, -(DT * edge_d) * ex, edge_u * hz)
            if x == LX - 1:
                show(16, edge_r * hz)
                ghost(16, (edge_r * edge_d) * ex, None)
            if x == 0:
                rz = edge_l * ey
                before = jnp.where(first8, 0.0, pltpu.roll(rz, 1, 1))
                show(17, -edge_l * ez)
                show(18, DT * ((rz - before) + edge_l * rise))
                show(19, DT * rz)
                ghost(18, None, -edge_u * rz)
        gat[s, me, 24:32, :] = (
            gho[0:8, :] + pltpu.roll(gho[8:16, :], 2, 1) + pltpu.roll(gho[16:24, :], 4, 1)
        )

    def gather_start(s):
        for copy in gather_copies(s):
            copy.start()

    def first_half(s, par, last):
        if last:
            for x in (0, 2):
                for cut in range(NCH):
                    local_h(par, x, cut)
        else:
            late_pack(s, par)

        @pl.when(s == 0)
        def _():
            for copy in loads[4:]:
                copy.wait()
            for x in range(LX):
                for cut in range(NCH):
                    z = pl.ds(cut * CH, CH)
                    region = rb[x, z, :]
                    rate = jnp.zeros((CH, LANES), F32)
                    for k in range(8):
                        rate = jnp.where(region == k, lvl[k], rate)
                    pump[x, z, :] = (DT * REC) * rate
                    gb[x, z, :] = SCALE * gi[x, z, :].astype(F32)

        def invert(cuts):
            @pl.when(s > 0)
            def _():
                for x in range(LX):
                    late_inversion(par, x, cuts)

        keep = jnp.where(s == 0, KEEP * DT, KEEP)
        invert((NCH - 1,))
        far_slab(s, par, keep)
        gather_start(s)
        if last:
            late_pack(s, par, True)
        invert(range(NCH - 1))
        for x in (0, 3, 1, 2):
            e_pass(par, x, keep)
        pl.when(s == 0)(build_tables)
        pl.when(s > 0)(lambda: add_batch(jnp.asarray(s - 1, jnp.int32)))


    def y_half(s, par):
        pl.when(has_u)(lambda: l1_copy(s).wait_recv())
        pl.when(has_d)(lambda: r1_copy(s).wait_recv())
        fix_y(s, par)


    def second_half(s, par, more):
        if more:
            early_pack(s + 1, 1 - par)

        pl.when(has_r & has_d)(lambda: r2_copy(s).wait_recv())
        pl.when(has_l & has_u)(lambda: l2_copy(s).wait_recv())

        def next_low(cut):
            if more:
                pl.when(has_l)(lambda: xe_copy(s + 1, 1 - par, cut).start())

        def next_high(cut):
            if more:
                outer_h(s + 1, 1 - par, cut)
                pl.when(has_r)(lambda: xh_copy(s + 1, cut).start())

        for cut in range(NCH - 1, -1, -1):
            pl.when(has_l)(lambda: xh_copy(s, cut).wait_recv())
            fix_first(s, par, cut)
            if cut > 0:
                next_low(cut)
            pl.when(has_r)(lambda: xe_copy(s, par, cut).wait_recv())
            if cut < NCH - 1:
                fix_outer(s, par, cut + 1)
            if 0 < cut < NCH - 1:
                next_high(cut + 1)
        fix_outer(s, par, 0)
        if more:
            send_corners(s + 1, 1 - par)
        next_low(0)
        next_high(1)
        next_high(0)

        @pl.when(has_l)
        def _():
            whole = eb.at[par, pl.ds(1, 2), 0, body, :]
            remote(whole, rxe.at[s, :, body_h, :], xe_s.at[s], xe_r.at[0], (left, gy)).wait_send()

        @pl.when(has_r)
        def _():
            remote(hs.at[s], rxh.at[s], xh_s.at[s], xh_r.at[0], (right, gy)).wait_send()

        pl.when(has_d)(lambda: l1_copy(s).wait_send())
        pl.when(has_u)(lambda: r1_copy(s).wait_send())
        pl.when(has_r & has_d)(lambda: l2_copy(s).wait_send())
        pl.when(has_l & has_u)(lambda: r2_copy(s).wait_send())
    def step(s, carry):
        s = jnp.asarray(s, jnp.int32)
        first_half(s, s % 2, False)
        y_half(s, s % 2)
        second_half(s, s % 2, True)
        return carry

    lax.fori_loop(0, STEPS - 1, step, 0)

    first_half(STEPS - 1, 1, True)
    add_batch(jnp.int32(STEPS - 1))

    col = lax.broadcasted_iota(jnp.int32, (48, LANES), 1)
    sign = jnp.where(col < 64, -1.0, 1.0)
    filler = jnp.zeros((16, LANES), F32)
    for f in range(FL):
        part = inn[:, f * LANES : (f + 1) * LANES]
        rhs = jnp.concatenate([part, filler, sign * pltpu.roll(part, 64, 1), filler], axis=0)
        res = dot3((xt_h[f], xt_l[f]), split(rhs))
        for d in range(16):
            sbuf[d, f] = res[8 * d : 8 * d + 8, :]

    scatter = [
        remote(sbuf.at[to], rbuf.at[dest], rs_s, rs_r, peer) for to, peer in scatter_peers()
    ]
    for copy in scatter:
        copy.start()
    rbuf[dest] = sbuf[dest]

    y_half(STEPS - 1, 1)
    second_half(STEPS - 1, 1, False)
    final = pltpu.make_async_copy(eb.at[0, :, :, body, :], out_e, out_sem)
    final.start()

    fifteen = pl.ds(0, 15)
    pltpu.make_async_copy(rbuf.at[fifteen], rbuf.at[fifteen], rs_r).wait()

    low_half = lax.broadcasted_iota(jnp.int32, (1, LANES), 1) < 64
    for f in range(FL):
        total = rbuf[0, f]
        for d in range(1, 16):
            total = total + rbuf[d, f]
        turned = pltpu.roll(total, 64, 1)
        for a in range(2):
            for pair in range(2):
                r0, r1 = a * 4 + 2 * pair, a * 4 + 2 * pair + 1
                real = jnp.where(low_half, total[r0 : r0 + 1, :], turned[r1 : r1 + 1, :])
                imag = jnp.where(low_half, turned[r0 : r0 + 1, :], total[r1 : r1 + 1, :])
                out_f[a, f : f + 1, pair * LANES : (pair + 1) * LANES] = real
                out_f[a, f : f + 1, 256 + pair * LANES : 256 + (pair + 1) * LANES] = imag

    pltpu.make_async_copy(sbuf.at[fifteen], sbuf.at[fifteen], rs_s).wait()

    def settle(n, carry):
        gather_wait(n, g_s)
        return carry

    lax.fori_loop(0, STEPS, settle, 0)
    final.wait()


def store(field, far, out_e, out_f, field_sem, far_sem):
    copies = [
        pltpu.make_async_copy(far, out_f, far_sem),
        pltpu.make_async_copy(field, out_e, field_sem),
    ]
    for copy in copies:
        copy.start()
    for copy in copies:
        copy.wait()


def local(electric, magnetic, polarization, current, inversion, gain_mask, pump_region, pump_level):
    anywhere = pl.BlockSpec(memory_space=pl.ANY)
    far_memory = pl.BlockSpec(memory_space=pltpu.HBM)
    near_memory = pl.BlockSpec(memory_space=pltpu.VMEM)
    dma = pltpu.SemaphoreType.DMA
    vmem = pltpu.VMEM
    state = (3, LX, NZ, LANES)
    operands = [
        pltpu.with_memory_space_constraint(operand, pltpu.HBM)
        for operand in (
            electric, magnetic, polarization, current, inversion, gain_mask, pump_region, pump_level,
        )
    ]
    field, far = pl.pallas_call(
        kernel,
        out_shape=(
            jax.ShapeDtypeStruct(state, F32),
            jax.ShapeDtypeStruct((2, FL, 512), F32),
        ),
        in_specs=[far_memory] * 8,
        out_specs=(near_memory, near_memory),
        scratch_shapes=[
            vmem((2, 3, LX, NZ + 8, LANES), F32),
            vmem((3, LX, NZ + 8, LANES), F32),
            vmem(state, F32),
            vmem(state, F32),
            vmem(state[1:], F32),
            vmem(state[1:], jnp.int32),
            vmem(state[1:], F32),
            vmem(state[1:], jnp.int32),
            vmem(state[1:], F32),
            vmem((STEPS, 2, NZ, LANES), F32),
            vmem((STEPS, 2, NZ + 8, LANES), F32),
            vmem((STEPS, 2, NZ, LANES), F32),
            vmem((STEPS, CH, LANES), F32),
            vmem((STEPS, CH, LANES), F32),
            vmem((STEPS, CH, LANES), F32),
            vmem((STEPS, CH, LANES), F32),
            vmem((STEPS, CH, LANES), F32),
            vmem((STEPS, CH, LANES), F32),
            vmem((STEPS, CH, LANES), F32),
            vmem((STEPS, CH, LANES), F32),
            vmem((STEPS, 8, 32, LANES), F32),
            vmem((24, LANES), F32),
            vmem((512, FL * LANES), BF16),
            vmem((512, FL * LANES), BF16),
            vmem((FL, 128, LANES), BF16),
            vmem((FL, 128, LANES), BF16),
            vmem((48, FL * LANES), F32),
            vmem((16, FL, 8, LANES), F32),
            vmem((16, FL, 8, LANES), F32),
            pltpu.SMEM((8,), F32),
            dma((10,)),
            dma((STEPS,)),
            dma((STEPS * NCH,)),
            dma((STEPS,)),
            dma((STEPS * NCH,)),
        ]
        + [dma((STEPS,))] * 10
        + [dma, dma, dma],
        compiler_params=pltpu.CompilerParams(
            collective_id=0, has_side_effects=True, vmem_limit_bytes=24 << 20
        ),
    )(*operands)
    return pl.pallas_call(
        store,
        out_shape=(
            jax.ShapeDtypeStruct(state, F32),
            jax.ShapeDtypeStruct((2, FL, 512), F32),
        ),
        in_specs=[anywhere] * 2,
        out_specs=(anywhere, anywhere),
        scratch_shapes=[dma, dma],
        compiler_params=pltpu.CompilerParams(vmem_limit_bytes=1 << 20),
    )(field, far)


def solution(mesh):
    return jax.shard_map(
        local,
        mesh=mesh,
        in_specs=(
            P(None, "gx", None, "gy"),
            P(None, "gx", None, "gy"),
            P(None, "gx", None, "gy"),
            P(None, "gx", None, "gy"),
            P("gx", None, "gy"),
            P("gx", None, "gy"),
            P("gx", None, "gy"),
            P(),
        ),
        out_specs=(P(None, "gx", None, "gy"), P("gx", "gy", None)),
        check_vma=False,
    )
```

```python
import functools
import math

import jax
import jax.numpy as jnp
from jax import lax
from jax.experimental import pallas as pl
from jax.experimental.pallas import tpu as pltpu
from jax.sharding import PartitionSpec as P

MESH = pl.DeviceIdType.MESH
F32 = jnp.float32
BF16 = jnp.bfloat16

STEPS = 4
NZ = 96
LX = 4
LANES = 128
CH = 32
NCH = NZ // CH
FL = 4

DT = 0.5
DAMP = 0.4
SAT = 0.5
REC = 0.8
SCALE = DT * DT / (1.0 + 0.5 * DAMP * DT)
KEEP = (1.0 - 0.5 * DAMP * DT) / (DT * DT)


def sin_turns(turns):
    r = turns - jnp.floor(turns + 0.5)
    x = r * (2.0 * math.pi)
    s = x * x
    acc = jnp.full_like(s, 1.0 / math.factorial(17))
    for order, sign in ((15, -1.0), (13, 1.0), (11, -1.0), (9, 1.0), (7, -1.0), (5, 1.0), (3, -1.0), (1, 1.0)):
        acc = acc * s + sign / math.factorial(order)
    return acc * x


def split(value):
    high = value.astype(BF16)
    return high, (value - high.astype(F32)).astype(BF16)


def dot3(a, b):
    ah, al = a
    bh, bl = b
    dot = functools.partial(jnp.dot, preferred_element_type=F32)
    return dot(ah, bh) + dot(al, bh) + dot(ah, bl)


def kernel(
    e_in, h_in, p_in, j_in, w_in, g_in, r_in, lvl_in,
    out_e, out_f,
    eb, hb, jb, pb, wb, gi, gb, rb, pump,
    hs, rxe, rxh, rye, ryh, rce, rch, sl, sr, tl, tr,
    gat, gho, tab_h, tab_l, xt_h, xt_l, inn, sbuf, rbuf,
    lvl, load_sem, xe_s, xe_r, xh_s, xh_r, l1_s, l2_s, r1_s, r2_s,
    ye_r, yh_r, ce_r, ch_r, g_s, g_r, rs_s, rs_r, out_sem,
):
    gx = lax.axis_index("gx")
    gy = lax.axis_index("gy")
    y_lo = gx // 16
    xc = (gx // 4) % 4
    zc = gx % 4
    left, right = (gx + 31) % 32, (gx + 1) % 32
    down, up = (gy + 3) % 4, (gy + 1) % 4
    has_l, has_r = gx > 0, gx < 31
    has_d, has_u = gy > 0, gy < 3
    dest = xc * 4 + zc

    def gather_peers():
        for dl in range(2):
            for dy in range(4):
                if dl or dy:
                    yield ((gx + 16 * dl) % 32, (gy + dy) % 4)

    def scatter_peers():
        for d in range(1, 16):
            to = (dest + d) % 16
            yield to, (y_lo * 16 + to, gy)

    def load(src, dst, index):
        return pltpu.make_async_copy(src, dst, load_sem.at[index])

    body, body_h = pl.ds(0, NZ), pl.ds(8, NZ)
    inner, outer = pl.ds(0, LX - 1), pl.ds(LX - 1, 1)
    loads = [
        load(e_in.at[:, outer], eb.at[0, :, outer, body, :], 0),
        load(h_in.at[:, outer], hb.at[:, outer, body_h, :], 1),
        load(e_in.at[:, inner], eb.at[0, :, inner, body, :], 2),
        load(h_in.at[:, inner], hb.at[:, inner, body_h, :], 3),
        load(j_in, jb, 4),
        load(p_in, pb, 5),
        load(w_in, wb, 6),
        load(g_in, gi, 7),
        load(r_in, rb, 8),
        load(lvl_in, lvl, 9),
    ]
    for copy in loads:
        copy.start()

    barrier = pltpu.get_barrier_semaphore()

    def greet(device):
        pl.semaphore_signal(barrier, inc=1, device_id=device, device_id_type=MESH)

    pl.when(has_l)(lambda: greet((left, gy)))
    pl.when(has_r)(lambda: greet((right, gy)))
    pl.when(has_l & has_u)(lambda: greet((left, up)))
    pl.when(has_r & has_d)(lambda: greet((right, down)))
    for peer in gather_peers():
        greet(peer)
    for _, peer in scatter_peers():
        greet(peer)

    gho[...] = jnp.zeros(gho.shape, F32)
    zero_row = jnp.zeros((8, LANES), F32)
    for c in range(3):
        for x in range(LX):
            eb[0, c, x, NZ:, :] = zero_row
            eb[1, c, x, NZ:, :] = zero_row
            hb[c, x, 0:8, :] = zero_row
    for step in range(STEPS):
        rxe[step, 1, 0:8, :] = zero_row

    @pl.when(jnp.logical_not(has_r))
    def _():
        rxe[...] = jnp.zeros(rxe.shape, F32)

    @pl.when(jnp.logical_not(has_l))
    def _():
        rxh[...] = jnp.zeros(rxh.shape, F32)

    @pl.when(jnp.logical_not(has_u))
    def _():
        rye[...] = jnp.zeros(rye.shape, F32)

    @pl.when(jnp.logical_not(has_d))
    def _():
        ryh[...] = jnp.zeros(ryh.shape, F32)

    @pl.when(jnp.logical_not(has_l & has_u))
    def _():
        rce[...] = jnp.zeros(rce.shape, F32)

    @pl.when(jnp.logical_not(has_r & has_d))
    def _():
        rch[...] = jnp.zeros(rch.shape, F32)

    edge_l = has_l.astype(F32) * DT
    edge_d = has_d.astype(F32) * DT
    edge_r = has_r.astype(F32) * DT
    edge_u = has_u.astype(F32) * DT
    lane = lax.broadcasted_iota(jnp.int32, (CH, LANES), 1)
    first_lane = lane == 0
    last_lane = lane == LANES - 1

    def remote(src, dst, send, recv, device):
        return pltpu.make_async_remote_copy(
            src_ref=src, dst_ref=dst, send_sem=send, recv_sem=recv,
            device_id=device, device_id_type=MESH,
        )

    def xe_copy(s, par, cut):
        z, zr = pl.ds(cut * CH, CH), pl.ds(8 + cut * CH, CH)
        return remote(
            eb.at[par, pl.ds(1, 2), 0, z, :], rxe.at[s, :, zr, :],
            xe_s.at[s], xe_r.at[s * NCH + cut], (left, gy),
        )

    def xh_copy(s, cut):
        z = pl.ds(cut * CH, CH)
        return remote(
            hs.at[s, :, z, :], rxh.at[s, :, z, :],
            xh_s.at[s], xh_r.at[s * NCH + cut], (right, gy),
        )

    def l1_copy(s):
        return remote(sl.at[s], rye.at[s], l1_s.at[s], ye_r.at[s], (gx, down))

    def l2_copy(s):
        return remote(tl.at[s], rce.at[s], l2_s.at[s], ce_r.at[s], (right, down))

    def r1_copy(s):
        return remote(sr.at[s], ryh.at[s], r1_s.at[s], yh_r.at[s], (gx, up))

    def r2_copy(s):
        return remote(tr.at[s], rch.at[s], r2_s.at[s], ch_r.at[s], (left, up))

    def local_h(par, x, cut):
        z = pl.ds(cut * CH, CH)
        z1 = pl.ds(cut * CH + 1, CH)
        zh = pl.ds(8 + cut * CH, CH)
        ex, ey, ez = eb[par, 0, x, z, :], eb[par, 1, x, z, :], eb[par, 2, x, z, :]
        exz, eyz = eb[par, 0, x, z1, :], eb[par, 1, x, z1, :]
        exy = jnp.where(last_lane, 0.0, pltpu.roll(ex, LANES - 1, 1))
        ezy = jnp.where(last_lane, 0.0, pltpu.roll(ez, LANES - 1, 1))
        hx = hb[0, x, zh, :] - DT * ((ezy - ez) - (eyz - ey))
        if x < LX - 1:
            hy = hb[1, x, zh, :] - DT * ((exz - ex) - (eb[par, 2, x + 1, z, :] - ez))
            hz = hb[2, x, zh, :] - DT * ((eb[par, 1, x + 1, z, :] - ey) - (exy - ex))
        else:
            hy = hb[1, x, zh, :] - DT * ((exz - ex) + ez)
            hz = hb[2, x, zh, :] + DT * (ey + (exy - ex))
        hb[0, x, zh, :] = hx
        hb[1, x, zh, :] = hy
        hb[2, x, zh, :] = hz
        if x == LX - 1:
            return hy, hz
        return hx, hz

    def outer_h(s, par, cut):
        z = pl.ds(cut * CH, CH)
        hs[s, 0, z, :], hs[s, 1, z, :] = local_h(par, LX - 1, cut)

    def turn(value, at, to):
        shift = (to - at) % LANES
        return pltpu.roll(value, shift, 1) if shift else value

    def put(acc, value, at, to):
        return jnp.where(lane == to, turn(value, at, to), acc)

    def drop_rate(x, z, drop):
        wb[x, z, :] = (1.0 - DT * REC) * wb[x, z, :] + pump[x, z, :] - (0.5 * SAT) * drop

    def e_pass(par, x, keep):
        for cut in range(NCH):
            z = pl.ds(cut * CH, CH)
            zh = pl.ds(8 + cut * CH, CH)
            zb = pl.ds(7 + cut * CH, CH)
            ex, ey, ez = eb[par, 0, x, z, :], eb[par, 1, x, z, :], eb[par, 2, x, z, :]
            hx, hy, hz = hb[0, x, zh, :], hb[1, x, zh, :], hb[2, x, zh, :]
            dy_hz = hz - jnp.where(first_lane, edge_d * ex, pltpu.roll(hz, 1, 1))
            dy_hx = hx + jnp.where(first_lane, edge_d * ez, -pltpu.roll(hx, 1, 1))
            if x == 0:
                dx_hz = hz + edge_l * ey
                dx_hy = hy - edge_l * ez
            else:
                dx_hz = hz - hb[2, x - 1, zh, :]
                dx_hy = hy - hb[1, x - 1, zh, :]
            curl_x = dy_hz - (hy - hb[1, x, zb, :])
            curl_y = (hx - hb[0, x, zb, :]) - dx_hz
            curl_z = dx_hy - dy_hx
            inv = wb[x, z, :]
            gain = gb[x, z, :]
            for c, old, curl in ((0, ex, curl_x), (1, ey, curl_y), (2, ez, curl_z)):
                pol = pb[c, x, z, :]
                cur = gain * (keep * jb[c, x, z, :] + (inv * old - pol))
                jb[c, x, z, :] = cur
                pb[c, x, z, :] = pol + cur
                eb[1 - par, c, x, z, :] = old + (DT * curl - cur)

    small_lane = lane % 16
    top_row = lax.broadcasted_iota(jnp.int32, (CH, LANES), 0) == 0
    edge_lanes = first_lane | last_lane

    def fix_y(s, par):
        ye, yh = rye[s], ryh[s]
        ye8, yh8 = pltpu.roll(ye, LANES - 8, 1), pltpu.roll(yh, LANES - 8, 1)
        under = pltpu.roll(ye8, 1, 0)
        under = jnp.where(top_row, jnp.where(lane < 16, 0.0, pltpu.roll(under, 16, 1)), under)
        before = jnp.where(small_lane >= 2, pltpu.roll(ye, 2, 1), 0.0)
        add_x = (DT * DT) * ye - DT * yh8
        add_y = (DT * DT) * ((before - ye) - (ye8 - under))
        add_z = (DT * DT) * ye8 + DT * yh
        new = 1 - par
        for x in (0, 3, 1, 2):
            for cut in range(NCH):
                z = pl.ds(cut * CH, CH)
                zh = pl.ds(8 + cut * CH, CH)
                at = cut * 16 + 2 * x
                eb[new, 0, x, z, :] = eb[new, 0, x, z, :] + jnp.where(edge_lanes, turn(add_x, at, LANES - 1), 0.0)
                eb[new, 1, x, z, :] = eb[new, 1, x, z, :] + jnp.where(last_lane, turn(add_y, at, LANES - 1), 0.0)
                eb[new, 2, x, z, :] = eb[new, 2, x, z, :] + jnp.where(edge_lanes, turn(add_z, at, LANES - 1), 0.0)
                hb[0, x, zh, :] = hb[0, x, zh, :] - jnp.where(last_lane, DT * turn(ye8, at, LANES - 1), 0.0)
                hb[2, x, zh, :] = hb[2, x, zh, :] + jnp.where(last_lane, DT * turn(ye, at, LANES - 1), 0.0)

    def late_inversion(par, x, cuts):
        for cut in cuts:
            z = pl.ds(cut * CH, CH)
            drop = None
            for c in range(3):
                term = (eb[par, c, x, z, :] + eb[1 - par, c, x, z, :]) * jb[c, x, z, :]
                drop = term if drop is None else drop + term
            drop_rate(x, z, drop)

    def fix_first(s, par, cut):
        z = pl.ds(cut * CH, CH)
        corner = jnp.where(last_lane, (DT * DT) * turn(rce[s], cut * 16, LANES - 1), 0.0)
        eb[1 - par, 1, 0, z, :] = eb[1 - par, 1, 0, z, :] + (DT * rxh[s, 1, z, :] + corner)
        eb[1 - par, 2, 0, z, :] = eb[1 - par, 2, 0, z, :] - DT * rxh[s, 0, z, :]

    def fix_outer(s, par, cut):
        x = LX - 1
        z = pl.ds(cut * CH, CH)
        zh = pl.ds(8 + cut * CH, CH)
        zb = pl.ds(7 + cut * CH, CH)
        ry = DT * rxe[s, 1, zh, :]
        rz = DT * rxe[s, 0, zh, :]
        hb[1, x, zh, :] = hb[1, x, zh, :] + ry
        hb[2, x, zh, :] = hb[2, x, zh, :] - rz
        side = jnp.where(first_lane, DT * turn(rch[s], cut * 16, 0), pltpu.roll(rz, 1, 1))
        back = DT * rxe[s, 1, zb, :]
        eb[1 - par, 0, x, z, :] = eb[1 - par, 0, x, z, :] + DT * ((side - rz) - (ry - back))
        eb[1 - par, 1, x, z, :] = eb[1 - par, 1, x, z, :] + DT * rz
        eb[1 - par, 2, x, z, :] = eb[1 - par, 2, x, z, :] + DT * ry

    def wave_turns(col):
        f = gy * FL + col // LANES
        return (0.6 + 0.05 * f.astype(F32)) * (1.0 / (2.0 * math.pi))

    def direction(index):
        return 0.75 * (2.0 * index.astype(F32) - 63.0) / 63.0

    def build_tables():
        rows = 64

        def y_rows(i, carry):
            row = lax.broadcasted_iota(jnp.int32, (rows, LANES), 0) + i * rows
            col = lax.broadcasted_iota(jnp.int32, (rows, LANES), 1)
            base = (row.astype(F32) - 256.0) * direction(col % 64)
            quarter = jnp.where(col < 64, 0.25, 0.0)
            for f in range(FL):
                wave = (0.6 + 0.05 * (gy * FL + f).astype(F32)) * (1.0 / (2.0 * math.pi))
                high, low = split(sin_turns(wave * base + quarter))
                tab_h[pl.ds(i * rows, rows), f * LANES : (f + 1) * LANES] = high
                tab_l[pl.ds(i * rows, rows), f * LANES : (f + 1) * LANES] = low
            return carry

        lax.fori_loop(0, 512 // rows, y_rows, 0)
        row = lax.broadcasted_iota(jnp.int32, (128, LANES), 0)
        col = lax.broadcasted_iota(jnp.int32, (128, LANES), 1)
        a = 2 * (y_lo * 16 + row // 8) + (row // 4) % 2
        item = col % 64
        group = jnp.where(item < 24, 0, 1)
        r = item - group * 24
        kind = jnp.where(r < 16, r // 4, jnp.where(r == 17, 0, jnp.where(r == 18, 3, 2)))
        place = jnp.where(r < 16, r % 4, jnp.where(r == 16, 4, -1))
        cell = (group * 16 + dest) * 4 + place - 64
        base = cell.astype(F32) * direction(a)
        quarter = jnp.where(col < 64, 0.25, 0.0)
        used = ((row % 4) == kind) & (item < 48) & (r < 20)
        for f in range(FL):
            wave = (0.6 + 0.05 * (gy * FL + f).astype(F32)) * (1.0 / (2.0 * math.pi))
            value = jnp.where(used, sin_turns(wave * base + quarter), 0.0) * (1.0 / 256.0)
            high, low = split(value)
            xt_h[f] = high
            xt_l[f] = low
        inn[...] = jnp.zeros(inn.shape, F32)

    gather_bytes = pl.ds(0, 7)

    def gather_copies(n):
        mine = gat.at[n, gy * 2 + y_lo]
        return [remote(mine, mine, g_s.at[n], g_r.at[n], peer) for peer in gather_peers()]

    def gather_wait(n, sem):
        pltpu.make_async_copy(gat.at[n, gather_bytes], gat.at[n, gather_bytes], sem.at[n]).wait()

    def add_batch(n):
        gather_wait(n, g_r)
        lane8 = lax.broadcasted_iota(jnp.int32, (8, LANES), 1)
        first8, last8 = lane8 == 0, lane8 == LANES - 1
        blocks = []
        for q in range(4):
            tiles = []
            for group in range(2):
                above = gat[n, (q + 1) * 2 + group, 24:32, :] if q < 3 else None
                below = gat[n, (q - 1) * 2 + group, 24:32, :] if q > 0 else None
                for t in range(3):
                    tile = gat[n, q * 2 + group, 8 * t : 8 * t + 8, :]
                    if above is not None:
                        tile = tile + jnp.where(last8, turn(above, 2 * t, 0), 0.0)
                    if below is not None:
                        tile = tile + jnp.where(first8, turn(below, 2 * t, 0), 0.0)
                    tiles.append(tile)
            blocks.append(jnp.concatenate(tiles, axis=0))
        lhs = jnp.concatenate(blocks, axis=1)
        res = dot3(split(lhs), (tab_h[...], tab_l[...]))
        row = lax.broadcasted_iota(jnp.int32, (24, LANES), 0)
        col = lax.broadcasted_iota(jnp.int32, (24, LANES), 1)
        late = jnp.where((row < 8) | (row == 17), 0.5, 1.0) + n.astype(F32)
        sign = jnp.where(col < 64, DT, -DT)
        for f in range(FL):
            wave = (0.6 + 0.05 * (gy * FL + f).astype(F32)) * (1.0 / (2.0 * math.pi))
            turns = wave * DT * late
            real = DT * sin_turns(turns + 0.25)
            imag = sign * sin_turns(turns)
            for group in range(2):
                part = res[group * 24 : (group + 1) * 24, f * LANES : (f + 1) * LANES]
                rows = pl.ds(group * 24, 24)
                inn[rows, f * LANES : (f + 1) * LANES] += real * part + imag * pltpu.roll(part, 64, 1)

    def pack_corners(s, par):
        left_col = jnp.zeros((CH, LANES), F32)
        right_col = jnp.zeros((CH, LANES), F32)
        for cut in range(NCH):
            z = pl.ds(cut * CH, CH)
            left_col = put(left_col, eb[par, 0, LX - 1, z, :], 0, cut * 16)
            right_col = put(right_col, eb[par, 1, 0, z, :], LANES - 1, cut * 16)
        tl[s] = left_col
        tr[s] = right_col

    def send_corners(s):
        pl.when(has_r & has_d)(lambda: l2_copy(s).start())
        pl.when(has_l & has_u)(lambda: r2_copy(s).start())

    loads[0].wait()
    loads[1].wait()
    for cut in range(NCH - 1, -1, -1):
        outer_h(0, 0, cut)
    loads[2].wait()
    pack_corners(0, 0)
    greeted = (
        22
        + has_l.astype(jnp.int32)
        + has_r.astype(jnp.int32)
        + (has_l & has_u).astype(jnp.int32)
        + (has_r & has_d).astype(jnp.int32)
    )
    pl.semaphore_wait(barrier, greeted)
    send_corners(0)

    @pl.when(has_l)
    def _():
        for cut in range(NCH - 1, -1, -1):
            xe_copy(0, 0, cut).start()

    @pl.when(has_r)
    def _():
        for cut in range(NCH - 1, -1, -1):
            xh_copy(0, cut).start()

    def put_low(pack, par, x):
        for cut in range(NCH):
            z = pl.ds(cut * CH, CH)
            pack = put(pack, eb[par, 0, x, z, :], 0, cut * 16 + 2 * x)
            pack = put(pack, eb[par, 2, x, z, :], 0, cut * 16 + 8 + 2 * x)
        return pack

    def put_high(pack, par, x, done=False):
        for cut in range(NCH):
            if x < LX - 1 and not done:
                hx, hz = local_h(par, x, cut)
            else:
                zh = pl.ds(8 + cut * CH, CH)
                hx, hz = hb[0, x, zh, :], hb[2, x, zh, :]
            pack = put(pack, hx, LANES - 1, cut * 16 + 2 * x + 1)
            pack = put(pack, hz, LANES - 1, cut * 16 + 8 + 2 * x + 1)
        return pack

    def early_pack(s, par):
        none = jnp.zeros((CH, LANES), F32)
        sl[s] = put_low(put_low(none, par, 1), par, 2)
        sr[s] = put_high(none, par, 1)

    def late_pack(s, par, done=False):
        sl[s] = put_low(put_low(sl[s], par, 0), par, 3)
        pl.when(has_d)(lambda: l1_copy(s).start())
        sr[s] = put_high(put_high(put_high(sr[s], par, 3), par, 0, done), par, 2, done)
        pl.when(has_u)(lambda: r1_copy(s).start())

    loads[3].wait()
    early_pack(0, 0)

    def far_slab(s, par, keep):
        me = gy * 2 + y_lo
        z, zl, zh, zb = pl.ds(NZ - 8, 8), pl.ds(NZ - 9, 8), pl.ds(NZ, 8), pl.ds(NZ - 1, 8)
        lane8 = lax.broadcasted_iota(jnp.int32, (8, LANES), 1)
        first8, last8 = lane8 == 0, lane8 == LANES - 1
        nothing = jnp.zeros((8, LANES), F32)

        def show(row, value):
            gat[s, me, row : row + 1, :] = value[7:8, :]

        def ghost(row, low, high):
            value = nothing
            if low is not None:
                value = jnp.where(last8, pltpu.roll(low, LANES - 1, 1), value)
            if high is not None:
                value = jnp.where(first8, pltpu.roll(high, 1, 1), value)
            gho[row : row + 1, :] = value[7:8, :]

        gat[s, me, 16:24, :] = nothing
        for x in range(LX):
            ex, ey, ez = eb[par, 0, x, z, :], eb[par, 1, x, z, :], eb[par, 2, x, z, :]
            hx, hy, hz = hb[0, x, zh, :], hb[1, x, zh, :], hb[2, x, zh, :]
            dy_hz = hz - jnp.where(first8, edge_d * ex, pltpu.roll(hz, 1, 1))
            dx_hz = hz + edge_l * ey if x == 0 else hz - hb[2, x - 1, zh, :]
            curl_x = dy_hz - (hy - hb[1, x, zb, :])
            curl_y = (hx - hb[0, x, zb, :]) - dx_hz
            inv, gain = wb[x, z, :], gb[x, z, :]
            cur_x = gain * (keep * jb[0, x, z, :] + (inv * ex - pb[0, x, z, :]))
            cur_y = gain * (keep * jb[1, x, z, :] + (inv * ey - pb[1, x, z, :]))
            show(x, -hy)
            show(4 + x, hx)
            show(8 + x, ey + (DT * curl_y - cur_y))
            show(12 + x, -(ex + (DT * curl_x - cur_x)))
            rise = ez - eb[par, 2, x, zl, :]
            side = -rise - ex if x == 0 else eb[par, 0, x - 1, z, :] - rise - ex
            ghost(4 + x, -edge_d * ez, None)
            ghost(8 + x, (DT * edge_d) * side, None)
            ghost(12 + x, -(DT * edge_d) * ex, edge_u * hz)
            if x == LX - 1:
                show(16, edge_r * hz)
                ghost(16, (edge_r * edge_d) * ex, None)
            if x == 0:
                rz = edge_l * ey
                before = jnp.where(first8, 0.0, pltpu.roll(rz, 1, 1))
                show(17, -edge_l * ez)
                show(18, DT * ((rz - before) + edge_l * rise))
                show(19, DT * rz)
                ghost(18, None, -edge_u * rz)
        gat[s, me, 24:32, :] = (
            gho[0:8, :] + pltpu.roll(gho[8:16, :], 2, 1) + pltpu.roll(gho[16:24, :], 4, 1)
        )

    def gather_start(s):
        for copy in gather_copies(s):
            copy.start()

    def first_half(s, par, last):
        if last:
            for x in (0, 2):
                for cut in range(NCH):
                    local_h(par, x, cut)
        else:
            late_pack(s, par)

        @pl.when(s == 0)
        def _():
            for copy in loads[4:]:
                copy.wait()
            for x in range(LX):
                for cut in range(NCH):
                    z = pl.ds(cut * CH, CH)
                    region = rb[x, z, :]
                    rate = jnp.zeros((CH, LANES), F32)
                    for k in range(8):
                        rate = jnp.where(region == k, lvl[k], rate)
                    pump[x, z, :] = (DT * REC) * rate
                    gb[x, z, :] = SCALE * gi[x, z, :].astype(F32)

        def invert(cuts):
            @pl.when(s > 0)
            def _():
                for x in range(LX):
                    late_inversion(par, x, cuts)

        keep = jnp.where(s == 0, KEEP * DT, KEEP)
        invert((NCH - 1,))
        far_slab(s, par, keep)
        gather_start(s)
        if last:
            late_pack(s, par, True)
        invert(range(NCH - 1))
        for x in (0, 3, 1, 2):
            e_pass(par, x, keep)
        pl.when(s == 0)(build_tables)
        pl.when(s > 0)(lambda: add_batch(jnp.asarray(s - 1, jnp.int32)))


    def y_half(s, par):
        pl.when(has_u)(lambda: l1_copy(s).wait_recv())
        pl.when(has_d)(lambda: r1_copy(s).wait_recv())
        fix_y(s, par)


    def second_half(s, par, more):
        if more:
            early_pack(s + 1, 1 - par)

        pl.when(has_r & has_d)(lambda: r2_copy(s).wait_recv())
        pl.when(has_l & has_u)(lambda: l2_copy(s).wait_recv())

        def next_low(cut):
            if more:
                pl.when(has_l)(lambda: xe_copy(s + 1, 1 - par, cut).start())

        def next_high(cut):
            if more:
                outer_h(s + 1, 1 - par, cut)
                pl.when(has_r)(lambda: xh_copy(s + 1, cut).start())

        for cut in range(NCH - 1, -1, -1):
            pl.when(has_l)(lambda: xh_copy(s, cut).wait_recv())
            fix_first(s, par, cut)
            if cut > 0:
                next_low(cut)
            pl.when(has_r)(lambda: xe_copy(s, par, cut).wait_recv())
            if cut < NCH - 1:
                fix_outer(s, par, cut + 1)
            if 0 < cut < NCH - 1:
                next_high(cut + 1)
        fix_outer(s, par, 0)
        if more:
            pack_corners(s + 1, 1 - par)
            send_corners(s + 1)
        next_low(0)
        next_high(1)
        next_high(0)

        @pl.when(has_l)
        def _():
            whole = eb.at[par, pl.ds(1, 2), 0, body, :]
            remote(whole, rxe.at[s, :, body_h, :], xe_s.at[s], xe_r.at[0], (left, gy)).wait_send()

        @pl.when(has_r)
        def _():
            remote(hs.at[s], rxh.at[s], xh_s.at[s], xh_r.at[0], (right, gy)).wait_send()

        pl.when(has_d)(lambda: l1_copy(s).wait_send())
        pl.when(has_u)(lambda: r1_copy(s).wait_send())
        pl.when(has_r & has_d)(lambda: l2_copy(s).wait_send())
        pl.when(has_l & has_u)(lambda: r2_copy(s).wait_send())
    def step(s, carry):
        s = jnp.asarray(s, jnp.int32)
        first_half(s, s % 2, False)
        y_half(s, s % 2)
        second_half(s, s % 2, True)
        return carry

    lax.fori_loop(0, STEPS - 1, step, 0)

    first_half(STEPS - 1, 1, True)
    add_batch(jnp.int32(STEPS - 1))

    col = lax.broadcasted_iota(jnp.int32, (48, LANES), 1)
    sign = jnp.where(col < 64, -1.0, 1.0)
    filler = jnp.zeros((16, LANES), F32)
    for f in range(FL):
        part = inn[:, f * LANES : (f + 1) * LANES]
        rhs = jnp.concatenate([part, filler, sign * pltpu.roll(part, 64, 1), filler], axis=0)
        res = dot3((xt_h[f], xt_l[f]), split(rhs))
        for d in range(16):
            sbuf[d, f] = res[8 * d : 8 * d + 8, :]

    scatter = [
        remote(sbuf.at[to], rbuf.at[dest], rs_s, rs_r, peer) for to, peer in scatter_peers()
    ]
    for copy in scatter:
        copy.start()
    rbuf[dest] = sbuf[dest]

    y_half(STEPS - 1, 1)
    second_half(STEPS - 1, 1, False)
    final = pltpu.make_async_copy(eb.at[0, :, :, body, :], out_e, out_sem)
    final.start()

    fifteen = pl.ds(0, 15)
    pltpu.make_async_copy(rbuf.at[fifteen], rbuf.at[fifteen], rs_r).wait()

    low_half = lax.broadcasted_iota(jnp.int32, (1, LANES), 1) < 64
    for f in range(FL):
        total = rbuf[0, f]
        for d in range(1, 16):
            total = total + rbuf[d, f]
        turned = pltpu.roll(total, 64, 1)
        for a in range(2):
            for pair in range(2):
                r0, r1 = a * 4 + 2 * pair, a * 4 + 2 * pair + 1
                real = jnp.where(low_half, total[r0 : r0 + 1, :], turned[r1 : r1 + 1, :])
                imag = jnp.where(low_half, turned[r0 : r0 + 1, :], total[r1 : r1 + 1, :])
                out_f[a, f : f + 1, pair * LANES : (pair + 1) * LANES] = real
                out_f[a, f : f + 1, 256 + pair * LANES : 256 + (pair + 1) * LANES] = imag

    pltpu.make_async_copy(sbuf.at[fifteen], sbuf.at[fifteen], rs_s).wait()

    def settle(n, carry):
        gather_wait(n, g_s)
        return carry

    lax.fori_loop(0, STEPS, settle, 0)
    final.wait()


def store(field, far, out_e, out_f, field_sem, far_sem):
    copies = [
        pltpu.make_async_copy(far, out_f, far_sem),
        pltpu.make_async_copy(field, out_e, field_sem),
    ]
    for copy in copies:
        copy.start()
    for copy in copies:
        copy.wait()


def local(electric, magnetic, polarization, current, inversion, gain_mask, pump_region, pump_level):
    anywhere = pl.BlockSpec(memory_space=pl.ANY)
    far_memory = pl.BlockSpec(memory_space=pltpu.HBM)
    near_memory = pl.BlockSpec(memory_space=pltpu.VMEM)
    dma = pltpu.SemaphoreType.DMA
    vmem = pltpu.VMEM
    state = (3, LX, NZ, LANES)
    operands = [
        pltpu.with_memory_space_constraint(operand, pltpu.HBM)
        for operand in (
            electric, magnetic, polarization, current, inversion, gain_mask, pump_region, pump_level,
        )
    ]
    field, far = pl.pallas_call(
        kernel,
        out_shape=(
            jax.ShapeDtypeStruct(state, F32),
            jax.ShapeDtypeStruct((2, FL, 512), F32),
        ),
        in_specs=[far_memory] * 8,
        out_specs=(near_memory, near_memory),
        scratch_shapes=[
            vmem((2, 3, LX, NZ + 8, LANES), F32),
            vmem((3, LX, NZ + 8, LANES), F32),
            vmem(state, F32),
            vmem(state, F32),
            vmem(state[1:], F32),
            vmem(state[1:], jnp.int32),
            vmem(state[1:], F32),
            vmem(state[1:], jnp.int32),
            vmem(state[1:], F32),
            vmem((STEPS, 2, NZ, LANES), F32),
            vmem((STEPS, 2, NZ + 8, LANES), F32),
            vmem((STEPS, 2, NZ, LANES), F32),
            vmem((STEPS, CH, LANES), F32),
            vmem((STEPS, CH, LANES), F32),
            vmem((STEPS, CH, LANES), F32),
            vmem((STEPS, CH, LANES), F32),
            vmem((STEPS, CH, LANES), F32),
            vmem((STEPS, CH, LANES), F32),
            vmem((STEPS, CH, LANES), F32),
            vmem((STEPS, CH, LANES), F32),
            vmem((STEPS, 8, 32, LANES), F32),
            vmem((24, LANES), F32),
            vmem((512, FL * LANES), BF16),
            vmem((512, FL * LANES), BF16),
            vmem((FL, 128, LANES), BF16),
            vmem((FL, 128, LANES), BF16),
            vmem((48, FL * LANES), F32),
            vmem((16, FL, 8, LANES), F32),
            vmem((16, FL, 8, LANES), F32),
            pltpu.SMEM((8,), F32),
            dma((10,)),
            dma((STEPS,)),
            dma((STEPS * NCH,)),
            dma((STEPS,)),
            dma((STEPS * NCH,)),
        ]
        + [dma((STEPS,))] * 10
        + [dma, dma, dma],
        compiler_params=pltpu.CompilerParams(
            collective_id=0, has_side_effects=True, vmem_limit_bytes=24 << 20
        ),
    )(*operands)
    return pl.pallas_call(
        store,
        out_shape=(
            jax.ShapeDtypeStruct(state, F32),
            jax.ShapeDtypeStruct((2, FL, 512), F32),
        ),
        in_specs=[anywhere] * 2,
        out_specs=(anywhere, anywhere),
        scratch_shapes=[dma, dma],
        compiler_params=pltpu.CompilerParams(vmem_limit_bytes=1 << 20),
    )(field, far)


def solution(mesh):
    return jax.shard_map(
        local,
        mesh=mesh,
        in_specs=(
            P(None, "gx", None, "gy"),
            P(None, "gx", None, "gy"),
            P(None, "gx", None, "gy"),
            P(None, "gx", None, "gy"),
            P("gx", None, "gy"),
            P("gx", None, "gy"),
            P("gx", None, "gy"),
            P(),
        ),
        out_specs=(P(None, "gx", None, "gy"), P("gx", "gy", None)),
        check_vma=False,
    )
```
